256 devices in a mesh: band: 4 (over y_lo, core), slab: 64 (over z, y_hi, x).
Axes of the slice: x: 4, y: 4 (y_hi: 2, y_lo: 2; y = y_hi * 2 + y_lo), z: 8, core: 2. Of those that a mesh axis runs over, the one named last changes fastest.
Arguments:
- bands: float32 [8, 192, 192, 192], P('band', 'slab'), may hold values from -8 to 8
- occupied: float32 [16, 192, 192, 192], P('band', 'slab'), may hold values from -8 to 8
- occ_index: int32 [2], replicated, may hold values from 0 to 15
- band_pick: int32 [8], P('band'), may hold values from 0 to 1
Outputs:
- exchange_out: float32 [8, 192, 192, 192], P('band', 'slab')
The draws below stay inside these ranges and needn't reach their ends.
All inputs are finite; a program needn't handle non-finite values.
Results may differ from the reference program's by a relative error of at most 0.0001.
Values sent between devices are 32-bit elements; how exact they have to be, the bound alone decides.
A program may use at most 64 MiB of HBM per device.

```python
import math
import jax
import jax.numpy as jnp
from jax import lax

NG = 192
BAND_DEV = 2
PAIR = 2
WIN = 2
BANDS = 8
OCC_ALL = 16
PICKS = 8


def orbital_values(key, count):
    shape = (count, NG, NG, NG)
    base = jnp.clip(jax.random.normal(key, shape, jnp.float32), -6.0, 6.0)
    return base


def draw_bands(key, part):
    return orbital_values(jax.random.fold_in(key, 11), BANDS)


def draw_occupied(key, part):
    return orbital_values(jax.random.fold_in(key, 23), OCC_ALL)


def place_ends(drawn, rng, low, high):
    longest = drawn.shape.index(max(drawn.shape))
    spots = []
    for shift in (0, 1):
        where = [jax.random.randint(jax.random.fold_in(rng, axis), (), 0, length) for axis, length in enumerate(drawn.shape)]
        where[longest] = (where[longest] + shift) % drawn.shape[longest]
        spots.append(tuple(where))
    return drawn.at[spots[0]].set(low).at[spots[1]].set(high)


def setup_inputs(seed: int = 0) -> dict:
    key_list = jax.random.split(jax.random.key(seed), 5)
    bands = draw_bands(jax.random.fold_in(key_list[4], 71), 0)
    occupied = draw_occupied(jax.random.fold_in(key_list[4], 71), 0)
    occ_index = jax.random.randint(key_list[2], (WIN,), 0, OCC_ALL).astype(jnp.int32)
    band_pick = place_ends(jax.random.randint(key_list[3], (PICKS,), 0, BAND_DEV), jax.random.fold_in(key_list[3], 1), 0, BAND_DEV - 1).astype(jnp.int32)
    return {"bands": bands, "occupied": occupied, "occ_index": occ_index, "band_pick": band_pick}


grid_step = 0.25
omega = 0.106


def wave_squared(length):
    modes = jnp.arange(length, dtype=jnp.int32)
    signed = jnp.where(modes <= length // 2, modes, modes - length)
    wave = (2.0 * math.pi / (length * grid_step)) * signed.astype(jnp.float32)
    return wave * wave


def screened(squares):
    nonzero = jnp.where(squares > 0, squares, jnp.ones_like(squares))
    value = 4.0 * math.pi * (1.0 - jnp.exp(-squares / (4.0 * omega * omega))) / nonzero
    return jnp.where(squares > 0, value, jnp.full_like(squares, math.pi / (omega * omega)))


def reference(bands, occupied, occ_index, band_pick):
    squares = wave_squared(NG)
    half_wave = squares[: NG // 2 + 1]
    kernel = screened(squares[:, None, None] + squares[None, :, None] + half_wave[None, None, :])
    rows = (jnp.arange(PICKS, dtype=jnp.int32) // PAIR) * BAND_DEV + band_pick.astype(jnp.int32)

    def one_row(row):
        target = lax.dynamic_index_in_dim(bands, row, 0, keepdims=False)

        def add_term(turn, total):
            which = occ_index[turn].astype(jnp.int32)
            orbital = lax.dynamic_index_in_dim(occupied, which, 0, keepdims=False)
            spectrum = jnp.fft.rfftn(orbital * target)
            potential = jnp.fft.irfftn(kernel * spectrum, s=(NG, NG, NG))
            return total - potential.astype(total.dtype) * orbital

        return lax.fori_loop(0, WIN, add_term, jnp.zeros((NG, NG, NG), bands.dtype))

    return lax.map(one_row, rows)
```

```python
import functools
import math

import jax
import jax.numpy as jnp
import numpy as np
from jax import lax
from jax.experimental import pallas as pl
from jax.experimental.pallas import tpu as pltpu
from jax.sharding import PartitionSpec as P

MESH = pl.DeviceIdType.MESH
F32, BF16 = jnp.float32, jnp.bfloat16
grid_step = 0.25
omega = 0.106
NG, SL, PL3, LN = 192, 64, 3, 128
ROWS, CUT = 56, 24


def split_host(matrix):
    high = matrix.astype(BF16)
    low = (matrix - high.astype(np.float64)).astype(BF16)
    return np.stack([np.asarray(high), np.asarray(low)])


def matrices():
    i = np.arange(NG)
    phase = 2.0 * np.pi / NG * ((i[:, None] * i[None, :]) % NG)
    cas = np.cos(phase) + np.sin(phase)
    first, second = np.zeros((256, 256)), np.zeros((256, 256))
    a, b, c = np.arange(128), np.arange(128, 192), np.arange(192, 256)
    pos0 = np.concatenate([a, b])
    pos1 = np.concatenate([a, c])
    first[np.ix_(pos0, pos0)] = cas
    second[np.ix_(pos1, pos1)] = cas
    order = (3 * np.arange(SL)[None, :] + np.arange(PL3)[:, None]).reshape(-1)
    across = cas[:, order]
    return [split_host(m) for m in (cas, np.stack([first, second]), across, across.T)]


def halves(v):
    high = v.astype(BF16)
    return high, (v - high.astype(F32)).astype(BF16)


def dot(a, b):
    return jnp.dot(a, b, preferred_element_type=F32)


def left(m_ref, v):
    high, low = halves(v)
    return dot(m_ref[0], high) + dot(m_ref[0], low) + dot(m_ref[1], high)


def along_z(b0, b1, b2, m_ref):
    (h0, l0), (h1, l1), (h2, l2) = halves(b0), halves(b1), halves(b2)

    def one(k, h, l):
        high, low = jnp.concatenate([h, h2], 1), jnp.concatenate([l, l2], 1)
        return dot(high, m_ref[0, k]) + dot(low, m_ref[0, k]) + dot(high, m_ref[1, k])

    r0, r1 = one(0, h0, l0), one(1, h1, l1)
    return r0[:, :LN], r1[:, :LN], r0[:, LN:] + r1[:, LN:]


def signed_square(mode):
    m = jnp.where(mode <= NG // 2, mode, mode - NG).astype(F32)
    wave = 2.0 * math.pi / (NG * grid_step) * m
    return wave * wave


def screened(squares):
    nonzero = jnp.where(squares > 0, squares, jnp.ones_like(squares))
    value = 4.0 * math.pi * (1.0 - jnp.exp(-squares / (4.0 * omega * omega))) / nonzero
    return jnp.where(squares > 0, value, jnp.full_like(squares, math.pi / (omega * omega)))


def kernel(
    occ_index, band_pick, bands, occupied, cas, zmat, xmat, xmat_t, out,
    send1, recv1, send2, recv2, own, got, part, cross, full, target, orb, table, acc,
    s1, r1, s2, r2, xs, xr,
):
    band, slab = lax.axis_index("band"), lax.axis_index("slab")
    y_lo, core = band // 2, band % 2
    zz, xy = slab // 8, slab % 8

    def peer(i):
        t, u = i % 8, i // 8
        dz = jnp.where(t % 2 == 1, (t + 1) // 2, 8 - t // 2)
        dxy = (u + t) % 8
        y, x = (xy // 4 + dxy // 4) % 2, (xy % 4 + dxy % 4) % 4
        return ((zz + dz) % 8) * 8 + y * 4 + x

    partner = {"band": y_lo * 2 + (1 - core)}
    across = {"band": (1 - y_lo) * 2 + core}
    barrier = pltpu.get_barrier_semaphore()

    def greet(i, carry):
        pl.semaphore_signal(barrier, inc=1, device_id={"slab": peer(i)}, device_id_type=MESH)
        return carry

    pl.semaphore_signal(barrier, inc=1, device_id=partner, device_id_type=MESH)
    pl.semaphore_signal(barrier, inc=1, device_id=across, device_id_type=MESH)
    lax.fori_loop(1, SL, greet, 0)

    for w in range(2):
        which = occ_index[w]
        mine = which // 4 == band
        for x in range(3):
            v = occupied[which % 4, x]
            v = jnp.where(mine, v, jnp.zeros_like(v))
            own[w, pl.ds(x * NG, NG), :] = v[:, :LN]
            high = v[:, LN:]
            own[w, pl.ds(576 + x * 96, 96), :] = jnp.concatenate([high[:96], high[96:]], 1)
    for x in range(3):
        t0, t1 = bands[band_pick[0], x], bands[band_pick[1], x]
        target[x, 0] = t0[:, :LN]
        target[x, 1] = t1[:, :LN]
        target[x, 2] = jnp.concatenate([t0[:, LN:], t1[:, LN:]], 1)

    pl.semaphore_wait(barrier, SL + 1)

    def hop(src, dst, k, where):
        return pltpu.make_async_remote_copy(
            src_ref=src, dst_ref=dst, send_sem=xs.at[k], recv_sem=xr.at[k], device_id=where, device_id_type=MESH
        )

    half = 432
    mine_rows = pl.ds(pl.multiple_of(core * half, 8), half)
    other_rows = pl.ds(pl.multiple_of((1 - core) * half, 8), half)
    first = [hop(own.at[w, other_rows], got.at[w], w, partner) for w in range(2)]
    second = [hop(part.at[w], cross.at[w], 2 + w, across) for w in range(2)]
    third = [hop(full.at[w, mine_rows], full.at[w, mine_rows], 4 + w, partner) for w in range(2)]
    first[0].start()
    first[1].start()
    for w in range(2):
        first[w].wait_recv()
        part[w] = own[w, mine_rows] + got[w]
        second[w].start()

    for j in range(3):
        ky = signed_square(jnp.full((NG, LN), j * SL, jnp.int32) + slab)
        kx = signed_square(lax.broadcasted_iota(jnp.int32, (NG, LN), 0))
        lane = lax.broadcasted_iota(jnp.int32, (NG, LN), 1)
        for b in range(2):
            kz = signed_square(lane if b == 0 else LN + lane % 64)
            table[j, b] = screened(kx + ky + kz) * (1.0 / float(NG * NG * NG))

    flat1, flat2 = send1.reshape(SL * ROWS, LN), send2.reshape(SL * ROWS, LN)
    in1, in2 = recv1.reshape(SL * ROWS, LN), recv2.reshape(SL * ROWS, LN)

    def rows_of(chunk):
        return pl.ds(0, CUT) if chunk == 0 else pl.ds(CUT, ROWS - CUT)

    def scatter(src, dst, ssem, rsem, chunk):
        rows = rows_of(chunk)

        def one(i, carry):
            d = peer(i)
            pltpu.make_async_remote_copy(
                src_ref=src.at[d, rows], dst_ref=dst.at[slab, rows], send_sem=ssem.at[chunk],
                recv_sem=rsem.at[chunk], device_id={"slab": d}, device_id_type=MESH,
            ).start()
            return carry

        lax.fori_loop(1, SL, one, 0)
        pltpu.make_async_copy(src.at[slab, rows], dst.at[slab, rows], rsem.at[chunk]).start()

    def arrived(dst, rsem, chunk):
        ref = dst.at[:, rows_of(chunk)]
        pltpu.make_async_copy(ref, ref, rsem.at[chunk]).wait()

    def sent(src, ssem, chunk):
        ref = src.at[pl.ds(0, SL - 1), rows_of(chunk)]
        pltpu.make_async_copy(ref, ref, ssem.at[chunk]).wait()

    low_lane = lax.broadcasted_iota(jnp.int32, (96, LN), 1) < 64
    for w in range(2):
        second[w].wait_recv()
        full[w, mine_rows] = part[w] + cross[w]
        third[w].start()
        third[w].wait_recv()
        for x in range(3):
            orb[w, x, 0] = full[w, pl.ds(x * NG, NG)]
            packed = full[w, pl.ds(576 + x * 96, 96)]
            turned = pltpu.roll(packed, 64, 1)
            orb[w, x, 1, :96] = jnp.where(low_lane, packed, turned)
            orb[w, x, 1, 96:] = jnp.where(low_lane, turned, packed)
        for x in range(3):
            o0, o1 = orb[w, x, 0], orb[w, x, 1]
            blocks = along_z(target[x, 0] * o0, target[x, 1] * o0, target[x, 2] * o1, zmat)
            for b in range(3):
                v = left(cas, blocks[b])
                for j in range(3):
                    n = w * 9 + j * 3 + b
                    flat1[pl.ds(n * 3 + x, SL, stride=ROWS), :] = v[j * SL : (j + 1) * SL]
        scatter(send1, recv1, s1, r1, w)

    for chunk in range(2):
        arrived(recv1, r1, chunk)
        for n in range(0, 8, 2) if chunk == 0 else range(8, 18, 2):
            cols = []
            for m in (n, n + 1):
                cols.append(jnp.concatenate([in1[pl.ds(m * 3 + x, SL, stride=ROWS), :] for x in range(3)], 0))
            v = left(xmat, jnp.concatenate(cols, 1))
            scale = [table[(m % 9) // 3, (m % 3) // 2] for m in (n, n + 1)]
            v = left(xmat_t, v * jnp.concatenate(scale, 1))
            for k, m in enumerate((n, n + 1)):
                for x in range(3):
                    flat2[pl.ds(m * 3 + x, SL, stride=ROWS), :] = v[x * SL : (x + 1) * SL, k * LN : (k + 1) * LN]
        scatter(send2, recv2, s2, r2, chunk)

    for chunk in range(2):
        arrived(recv2, r2, chunk)
    for x in range(3):
        for w in range(2):
            blocks = []
            for b in range(3):
                rows = [in2[pl.ds((w * 9 + j * 3 + b) * 3 + x, SL, stride=ROWS), :] for j in range(3)]
                blocks.append(left(cas, jnp.concatenate(rows, 0)))
            blocks = along_z(*blocks, zmat)
            o0, o1 = orb[w, x, 0], orb[w, x, 1]
            for b, o in enumerate((o0, o0, o1)):
                acc[b] = -blocks[b] * o if w == 0 else acc[b] - blocks[b] * o
        for p in range(2):
            out[p, x] = jnp.concatenate([acc[p], acc[2][:, p * 64 : (p + 1) * 64]], 1)

    for w in range(2):
        first[w].wait_send()
        second[w].wait_send()
        third[w].wait_send()
        sent(send1, s1, w)
        sent(send2, s2, w)


def shards(bands, occupied, occ_index, band_pick):
    vmem, smem = pl.BlockSpec(memory_space=pltpu.VMEM), pl.BlockSpec(memory_space=pltpu.SMEM)
    big = pltpu.VMEM((SL, ROWS, LN), F32)
    return pl.pallas_call(
        kernel,
        out_shape=jax.ShapeDtypeStruct((2, PL3, NG, NG), F32),
        in_specs=[smem, smem] + [vmem] * 6,
        out_specs=vmem,
        scratch_shapes=[
            big, big, big, big,
            pltpu.VMEM((2, 864, LN), F32),
            pltpu.VMEM((2, 432, LN), F32),
            pltpu.VMEM((2, 432, LN), F32),
            pltpu.VMEM((2, 432, LN), F32),
            pltpu.VMEM((2, 864, LN), F32),
            pltpu.VMEM((PL3, 3, NG, LN), F32),
            pltpu.VMEM((2, PL3, 2, NG, LN), F32),
            pltpu.VMEM((3, 2, NG, LN), F32),
            pltpu.VMEM((3, NG, LN), F32),
            pltpu.SemaphoreType.DMA((2,)),
            pltpu.SemaphoreType.DMA((2,)),
            pltpu.SemaphoreType.DMA((2,)),
            pltpu.SemaphoreType.DMA((2,)),
            pltpu.SemaphoreType.DMA((6,)),
            pltpu.SemaphoreType.DMA((6,)),
        ],
        compiler_params=pltpu.CompilerParams(
            collective_id=0, has_side_effects=True, vmem_limit_bytes=48 * 1024 * 1024
        ),
    )(occ_index, band_pick, bands, occupied, *(jnp.asarray(m) for m in matrices()))


def solution(mesh):
    placed = (P("band", "slab", None, None), P("band", "slab", None, None), P(), P("band"))
    return jax.shard_map(
        shards, mesh=mesh, in_specs=placed, out_specs=P("band", "slab", None, None), check_vma=False
    )
```

```python
import functools
import math

import jax
import jax.numpy as jnp
import numpy as np
from jax import lax
from jax.experimental import pallas as pl
from jax.experimental.pallas import tpu as pltpu
from jax.sharding import PartitionSpec as P

MESH = pl.DeviceIdType.MESH
F32, BF16 = jnp.float32, jnp.bfloat16
grid_step = 0.25
omega = 0.106
NG, SL, PL3, LN = 192, 64, 3, 128
ROWS = 56
CHUNKS = ((0, 24), (24, 16), (40, 16))
BLOCKS = (range(0, 8), range(8, 13), range(13, 18))
Z_STEPS = (1, 7, 2, 6, 3, 5, 4)
XY_STEPS = ((0, 1), (0, 3), (1, 0), (0, 2), (1, 1), (1, 3), (1, 2))


def row_of(n, x):
    return n * 3 + x + (1 if n >= 13 else 0)


def split_host(matrix):
    high = matrix.astype(BF16)
    low = (matrix - high.astype(np.float64)).astype(BF16)
    return np.stack([np.asarray(high), np.asarray(low)])


def matrices():
    i = np.arange(NG)
    phase = 2.0 * np.pi / NG * ((i[:, None] * i[None, :]) % NG)
    cas = np.cos(phase) + np.sin(phase)
    first, second = np.zeros((256, 256)), np.zeros((256, 256))
    a, b, c = np.arange(128), np.arange(128, 192), np.arange(192, 256)
    pos0 = np.concatenate([a, b])
    pos1 = np.concatenate([a, c])
    first[np.ix_(pos0, pos0)] = cas
    second[np.ix_(pos1, pos1)] = cas
    order = (3 * np.arange(SL)[None, :] + np.arange(PL3)[:, None]).reshape(-1)
    across = cas[:, order]
    return [split_host(m) for m in (cas, np.stack([first, second]), across, across.T)]


def halves(v):
    high = v.astype(BF16)
    return high, (v - high.astype(F32)).astype(BF16)


def dot(a, b):
    return jnp.dot(a, b, preferred_element_type=F32)


def left(m_ref, v):
    high, low = halves(v)
    return dot(m_ref[0], high) + dot(m_ref[0], low) + dot(m_ref[1], high)


def along_z(b0, b1, b2, m_ref):
    (h0, l0), (h1, l1), (h2, l2) = halves(b0), halves(b1), halves(b2)

    def one(k, h, l):
        high, low = jnp.concatenate([h, h2], 1), jnp.concatenate([l, l2], 1)
        return dot(high, m_ref[0, k]) + dot(low, m_ref[0, k]) + dot(high, m_ref[1, k])

    r0, r1 = one(0, h0, l0), one(1, h1, l1)
    return r0[:, :LN], r1[:, :LN], r0[:, LN:] + r1[:, LN:]


def signed_square(mode):
    m = jnp.where(mode <= NG // 2, mode, mode - NG).astype(F32)
    wave = 2.0 * math.pi / (NG * grid_step) * m
    return wave * wave


def screened(squares):
    nonzero = jnp.where(squares > 0, squares, jnp.ones_like(squares))
    value = 4.0 * math.pi * (1.0 - jnp.exp(-squares / (4.0 * omega * omega))) / nonzero
    return jnp.where(squares > 0, value, jnp.full_like(squares, math.pi / (omega * omega)))


def kernel(
    occ_index, band_pick, bands_in, occupied_in, cas_in, zmat_in, xmat_in, xmat_t_in, out,
    send1, mid1, recv1, send2, mid2, recv2, own, got, part, cross, full, target, orb, table, acc,
    bands, occupied, cas, zmat, xmat, xmat_t,
    load, s_sem, r_sem, xs, xr,
):
    band, slab = lax.axis_index("band"), lax.axis_index("slab")
    y_lo, core = band // 2, band % 2
    zz, xy = slab // 8, slab % 8
    pairs = (
        (occupied_in, occupied), (bands_in, bands), (cas_in, cas), (zmat_in, zmat), (xmat_in, xmat), (xmat_t_in, xmat_t)
    )
    loads = [pltpu.make_async_copy(src, dst, load.at[k]) for k, (src, dst) in enumerate(pairs)]
    for copy in loads:
        copy.start()

    z_peers = [(zz + d) % 8 for d in Z_STEPS]
    xy_peers = [((xy // 4 + dy) % 2) * 4 + (xy % 4 + dx) % 4 for dy, dx in XY_STEPS]
    partner = {"band": y_lo * 2 + (1 - core)}
    across = {"band": (1 - y_lo) * 2 + core}
    barrier = pltpu.get_barrier_semaphore()
    for where in [partner, across] + [{"slab": z * 8 + xy} for z in z_peers] + [{"slab": zz * 8 + p} for p in xy_peers]:
        pl.semaphore_signal(barrier, inc=1, device_id=where, device_id_type=MESH)

    def pack(w):
        which = occ_index[w]
        mine = which // 4 == band
        for x in range(3):
            v = occupied[which % 4, x]
            v = jnp.where(mine, v, jnp.zeros_like(v))
            own[w, x, :NG] = v[:, :LN]
            high = v[:, LN:]
            own[w, x, NG:] = jnp.concatenate([high[:96], high[96:]], 1)

    def hop(src, dst, k, where):
        return pltpu.make_async_remote_copy(
            src_ref=src, dst_ref=dst, send_sem=xs.at[k], recv_sem=xr.at[k], device_id=where, device_id_type=MESH
        )

    half = 144
    mine_rows = pl.ds(pl.multiple_of(core * half, 8), half)
    other_rows = pl.ds(pl.multiple_of((1 - core) * half, 8), half)
    units = [(w, x) for w in range(2) for x in range(3)]
    first = [hop(own.at[w, x, other_rows], got.at[w, x], w * 3 + x, partner) for w, x in units]
    second = [hop(part.at[w, x], cross.at[w, x], 6 + w * 3 + x, across) for w, x in units]
    third = [hop(full.at[w, x, mine_rows], full.at[w, x, mine_rows], 12 + w * 3 + x, partner) for w, x in units]

    loads[0].wait()
    pack(0)
    pl.semaphore_wait(barrier, 16)
    for k in range(3):
        first[k].start()
    pack(1)
    for k in range(3, 6):
        first[k].start()
    for k, (w, x) in enumerate(units):
        first[k].wait_recv()
        part[w, x] = own[w, x, mine_rows] + got[w, x]
        second[k].start()

    loads[1].wait()
    for x in range(3):
        t0, t1 = bands[band_pick[0], x], bands[band_pick[1], x]
        target[x, 0] = t0[:, :LN]
        target[x, 1] = t1[:, :LN]
        target[x, 2] = jnp.concatenate([t0[:, LN:], t1[:, LN:]], 1)
    for copy in loads[2:]:
        copy.wait()

    for j in range(3):
        ky = signed_square(jnp.full((NG, LN), j * SL, jnp.int32) + slab)
        kx = signed_square(lax.broadcasted_iota(jnp.int32, (NG, LN), 0))
        lane = lax.broadcasted_iota(jnp.int32, (NG, LN), 1)
        for b in range(2):
            kz = signed_square(lane if b == 0 else LN + lane % 64)
            table[j, b] = screened(kx + ky + kz) * (1.0 / float(NG * NG * NG))

    flat1, in1, flat2, in2 = (r.reshape(SL * ROWS, LN) for r in (send1, recv1, send2, recv2))

    def exchange(src, dst, phase, chunk, along_zz):
        rows = pl.ds(*CHUNKS[chunk])
        k = phase * 3 + chunk
        for p in z_peers if along_zz else xy_peers:
            pltpu.make_async_remote_copy(
                src_ref=src.at[p, :, rows] if along_zz else src.at[:, p, rows],
                dst_ref=dst.at[zz, :, rows] if along_zz else dst.at[:, xy, rows],
                send_sem=s_sem.at[k], recv_sem=r_sem.at[k],
                device_id={"slab": p * 8 + xy if along_zz else zz * 8 + p}, device_id_type=MESH,
            ).start()
        if along_zz:
            pltpu.make_async_copy(src.at[zz, :, rows], dst.at[zz, :, rows], r_sem.at[k]).start()
        else:
            pltpu.make_async_copy(src.at[:, xy, rows], dst.at[:, xy, rows], r_sem.at[k]).start()

    def arrived(dst, phase, chunk):
        ref = dst.at[:, :, pl.ds(*CHUNKS[chunk])]
        pltpu.make_async_copy(ref, ref, r_sem.at[phase * 3 + chunk]).wait()

    def sent(src, phase, chunk):
        ref = src.at[pl.ds(0, 7), :, pl.ds(*CHUNKS[chunk])]
        pltpu.make_async_copy(ref, ref, s_sem.at[phase * 3 + chunk]).wait()

    low_lane = lax.broadcasted_iota(jnp.int32, (96, LN), 1) < 64

    def join(k):
        w, x = units[k]
        second[k].wait_recv()
        full[w, x, mine_rows] = part[w, x] + cross[w, x]
        third[k].start()

    def forward(k):
        w, x = units[k]
        third[k].wait_recv()
        orb[w, x, 0] = full[w, x, :NG]
        packed = full[w, x, NG:]
        turned = pltpu.roll(packed, 64, 1)
        orb[w, x, 1, :96] = jnp.where(low_lane, packed, turned)
        orb[w, x, 1, 96:] = jnp.where(low_lane, turned, packed)
        o0, o1 = orb[w, x, 0], orb[w, x, 1]
        blocks = along_z(target[x, 0] * o0, target[x, 1] * o0, target[x, 2] * o1, zmat)
        for b in range(3):
            v = left(cas, blocks[b])
            for j in range(3):
                flat1[pl.ds(row_of(w * 9 + j * 3 + b, x), SL, stride=ROWS), :] = v[j * SL : (j + 1) * SL]

    def middle(chunk):
        blocks = list(BLOCKS[chunk])
        for group in [blocks[i : i + 2] for i in range(0, len(blocks), 2)]:
            cols = [
                jnp.concatenate([in1[pl.ds(row_of(n, x), SL, stride=ROWS), :] for x in range(3)], 0) for n in group
            ]
            scale = [table[(n % 9) // 3, (n % 3) // 2] for n in group]
            v = left(xmat, jnp.concatenate(cols, 1))
            v = left(xmat_t, v * jnp.concatenate(scale, 1))
            for k, n in enumerate(group):
                for x in range(3):
                    flat2[pl.ds(row_of(n, x), SL, stride=ROWS), :] = v[x * SL : (x + 1) * SL, k * LN : (k + 1) * LN]

    def finish(w, x):
        blocks = []
        for b in range(3):
            rows = [in2[pl.ds(row_of(w * 9 + j * 3 + b, x), SL, stride=ROWS), :] for j in range(3)]
            blocks.append(left(cas, jnp.concatenate(rows, 0)))
        blocks = along_z(*blocks, zmat)
        o0, o1 = orb[w, x, 0], orb[w, x, 1]
        for b, o in enumerate((o0, o0, o1)):
            acc[x, b] = -blocks[b] * o if w == 0 else acc[x, b] - blocks[b] * o

    join(0)
    for k in range(6):
        if k < 5:
            join(k + 1)
        forward(k)
        if k == 2:
            exchange(send1, mid1, 0, 0, True)
    exchange(send1, mid1, 0, 1, True)
    exchange(send1, mid1, 0, 2, True)

    def relay1(chunk):
        arrived(mid1, 0, chunk)
        exchange(mid1, recv1, 1, chunk, False)

    def conv(chunk):
        arrived(recv1, 1, chunk)
        middle(chunk)
        exchange(send2, mid2, 2, chunk, False)

    def relay2(chunk):
        arrived(mid2, 2, chunk)
        exchange(mid2, recv2, 3, chunk, True)

    relay1(0)
    conv(0)
    relay1(1)
    conv(1)
    relay2(0)
    relay1(2)
    relay2(1)
    conv(2)
    relay2(2)
    arrived(recv2, 3, 0)
    arrived(recv2, 3, 1)
    for x in range(3):
        finish(0, x)
    arrived(recv2, 3, 2)
    for x in range(3):
        finish(1, x)
        for p in range(2):
            out[p, x] = jnp.concatenate([acc[x, p], acc[x, 2][:, p * 64 : (p + 1) * 64]], 1)

    for k in range(6):
        first[k].wait_send()
        second[k].wait_send()
        third[k].wait_send()
    for phase, src in enumerate((send1, mid1, send2, mid2)):
        for chunk in range(3):
            sent(src, phase, chunk)


def shards(bands, occupied, occ_index, band_pick):
    vmem, smem = pl.BlockSpec(memory_space=pltpu.VMEM), pl.BlockSpec(memory_space=pltpu.SMEM)
    constants = [jnp.asarray(m) for m in matrices()]
    arrays = [occupied, bands] + constants
    big = pltpu.VMEM((8, 8, ROWS, LN), F32)
    return pl.pallas_call(
        kernel,
        out_shape=jax.ShapeDtypeStruct((2, PL3, NG, NG), F32),
        in_specs=[smem, smem] + [pl.BlockSpec(memory_space=pl.ANY)] * 6,
        out_specs=vmem,
        scratch_shapes=[
            big, big, big, big, big, big,
            pltpu.VMEM((2, 3, 288, LN), F32),
            pltpu.VMEM((2, 3, 144, LN), F32),
            pltpu.VMEM((2, 3, 144, LN), F32),
            pltpu.VMEM((2, 3, 144, LN), F32),
            pltpu.VMEM((2, 3, 288, LN), F32),
            pltpu.VMEM((PL3, 3, NG, LN), F32),
            pltpu.VMEM((2, PL3, 2, NG, LN), F32),
            pltpu.VMEM((3, 2, NG, LN), F32),
            pltpu.VMEM((3, 3, NG, LN), F32),
            pltpu.VMEM(bands.shape, F32),
            pltpu.VMEM(occupied.shape, F32),
            *(pltpu.VMEM(m.shape, BF16) for m in constants),
            pltpu.SemaphoreType.DMA((6,)),
            pltpu.SemaphoreType.DMA((12,)),
            pltpu.SemaphoreType.DMA((12,)),
            pltpu.SemaphoreType.DMA((18,)),
            pltpu.SemaphoreType.DMA((18,)),
        ],
        compiler_params=pltpu.CompilerParams(
            collective_id=0, has_side_effects=True, vmem_limit_bytes=62 * 1024 * 1024
        ),
    )(occ_index, band_pick, bands, occupied, *constants)


def solution(mesh):
    placed = (P("band", "slab", None, None), P("band", "slab", None, None), P(), P("band"))
    return jax.shard_map(
        shards, mesh=mesh, in_specs=placed, out_specs=P("band", "slab", None, None), check_vma=False
    )
```

```python
import functools
import math

import jax
import jax.numpy as jnp
import numpy as np
from jax import lax
from jax.experimental import pallas as pl
from jax.experimental.pallas import tpu as pltpu
from jax.sharding import PartitionSpec as P

MESH = pl.DeviceIdType.MESH
F32, BF16 = jnp.float32, jnp.bfloat16
grid_step = 0.25
omega = 0.106
NG, SL, PL3, LN = 192, 64, 3, 128
ROWS = 56
CHUNKS = ((0, 24), (24, 16), (40, 16))
BLOCKS = (range(0, 8), range(8, 13), range(13, 18))
Z_STEPS = (1, 7, 2, 6, 3, 5, 4)
XY_STEPS = ((0, 1), (1, 3), (0, 0), (1, 0), (0, 3), (1, 1), (0, 2), (1, 2))


def row_of(n, x):
    return n * 3 + x + (1 if n >= 13 else 0)


def split_host(matrix):
    high = matrix.astype(BF16)
    low = (matrix - high.astype(np.float64)).astype(BF16)
    return np.stack([np.asarray(high), np.asarray(low)])


def matrices():
    i = np.arange(NG)
    phase = 2.0 * np.pi / NG * ((i[:, None] * i[None, :]) % NG)
    cas = np.cos(phase) + np.sin(phase)
    first, second = np.zeros((256, 256)), np.zeros((256, 256))
    a, b, c = np.arange(128), np.arange(128, 192), np.arange(192, 256)
    pos0 = np.concatenate([a, b])
    pos1 = np.concatenate([a, c])
    first[np.ix_(pos0, pos0)] = cas
    second[np.ix_(pos1, pos1)] = cas
    order = (3 * np.arange(SL)[None, :] + np.arange(PL3)[:, None]).reshape(-1)
    across = cas[:, order]
    return [split_host(m) for m in (cas, np.stack([first, second]), across, across.T)]


def halves(v):
    high = v.astype(BF16)
    return high, (v - high.astype(F32)).astype(BF16)


def dot(a, b):
    return jnp.dot(a, b, preferred_element_type=F32)


def left(m_ref, v):
    high, low = halves(v)
    return dot(m_ref[0], high) + dot(m_ref[0], low) + dot(m_ref[1], high)


def along_z(b0, b1, b2, m_ref):
    (h0, l0), (h1, l1), (h2, l2) = halves(b0), halves(b1), halves(b2)

    def one(k, h, l):
        high, low = jnp.concatenate([h, h2], 1), jnp.concatenate([l, l2], 1)
        return dot(high, m_ref[0, k]) + dot(low, m_ref[0, k]) + dot(high, m_ref[1, k])

    r0, r1 = one(0, h0, l0), one(1, h1, l1)
    return r0[:, :LN], r1[:, :LN], r0[:, LN:] + r1[:, LN:]


def signed_square(mode):
    m = jnp.where(mode <= NG // 2, mode, mode - NG).astype(F32)
    wave = 2.0 * math.pi / (NG * grid_step) * m
    return wave * wave


def screened(squares):
    nonzero = jnp.where(squares > 0, squares, jnp.ones_like(squares))
    value = 4.0 * math.pi * (1.0 - jnp.exp(-squares / (4.0 * omega * omega))) / nonzero
    return jnp.where(squares > 0, value, jnp.full_like(squares, math.pi / (omega * omega)))


def kernel(
    occ_index, band_pick, bands_in, occupied_in, cas_in, zmat_in, xmat_in, xmat_t_in, out,
    send1, mid1, recv1, send2, mid2, recv2, own, got, part, cross, full, target, orb, table, acc,
    bands, occupied, cas, zmat, xmat, xmat_t,
    load, s_sem, r_sem, xs, xr,
):
    band, slab = lax.axis_index("band"), lax.axis_index("slab")
    y_lo, core = band // 2, band % 2
    zz, xy = slab // 8, slab % 8
    pairs = (
        (occupied_in, occupied), (bands_in, bands), (cas_in, cas), (zmat_in, zmat), (xmat_in, xmat), (xmat_t_in, xmat_t)
    )
    loads = [pltpu.make_async_copy(src, dst, load.at[k]) for k, (src, dst) in enumerate(pairs)]
    for copy in loads:
        copy.start()

    z_peers = [(zz + d) % 8 for d in Z_STEPS]
    xy_peers = [((xy // 4 + dy) % 2) * 4 + (xy % 4 + dx) % 4 for dy, dx in XY_STEPS]
    partner = {"band": y_lo * 2 + (1 - core)}
    across = {"band": (1 - y_lo) * 2 + core}
    barrier = pltpu.get_barrier_semaphore()
    for where in [partner] + [{"slab": z * 8 + xy} for z in z_peers] + [{**across, "slab": zz * 8 + p} for p in xy_peers]:
        pl.semaphore_signal(barrier, inc=1, device_id=where, device_id_type=MESH)

    def pack(w):
        which = occ_index[w]
        mine = which // 4 == band
        for x in range(3):
            v = occupied[which % 4, x]
            v = jnp.where(mine, v, jnp.zeros_like(v))
            own[w, x, :NG] = v[:, :LN]
            high = v[:, LN:]
            own[w, x, NG:] = jnp.concatenate([high[:96], high[96:]], 1)

    def hop(src, dst, k, where):
        return pltpu.make_async_remote_copy(
            src_ref=src, dst_ref=dst, send_sem=xs.at[k], recv_sem=xr.at[k], device_id=where, device_id_type=MESH
        )

    half = 144
    mine_rows = pl.ds(pl.multiple_of(core * half, 8), half)
    other_rows = pl.ds(pl.multiple_of((1 - core) * half, 8), half)
    units = [(w, x) for w in range(2) for x in range(3)]
    first = [hop(own.at[w, x, other_rows], got.at[w, x], w * 3 + x, partner) for w, x in units]
    second = [hop(part.at[w, x], cross.at[w, x], 6 + w * 3 + x, across) for w, x in units]
    third = [hop(full.at[w, x, mine_rows], full.at[w, x, mine_rows], 12 + w * 3 + x, partner) for w, x in units]

    loads[0].wait()
    pack(0)
    pl.semaphore_wait(barrier, 16)
    for k in range(3):
        first[k].start()
    pack(1)
    for k in range(3, 6):
        first[k].start()
    for k, (w, x) in enumerate(units):
        first[k].wait_recv()
        part[w, x] = own[w, x, mine_rows] + got[w, x]
        second[k].start()

    loads[1].wait()
    for x in range(3):
        t0, t1 = bands[band_pick[0], x], bands[band_pick[1], x]
        target[x, 0] = t0[:, :LN]
        target[x, 1] = t1[:, :LN]
        target[x, 2] = jnp.concatenate([t0[:, LN:], t1[:, LN:]], 1)
    for copy in loads[2:]:
        copy.wait()

    for j in range(3):
        ky = signed_square(jnp.full((NG, LN), j * SL, jnp.int32) + slab)
        kx = signed_square(lax.broadcasted_iota(jnp.int32, (NG, LN), 0))
        lane = lax.broadcasted_iota(jnp.int32, (NG, LN), 1)
        for b in range(2):
            kz = signed_square(lane if b == 0 else LN + lane % 64)
            table[j, b] = screened(kx + ky + kz) * (1.0 / float(NG * NG * NG))

    flat1, in1, flat2, in2 = (r.reshape(SL * ROWS, LN) for r in (send1, recv1, send2, recv2))

    def exchange(src, dst, phase, chunk, along_zz):
        rows = pl.ds(*CHUNKS[chunk])
        k = phase * 3 + chunk
        for p in z_peers if along_zz else xy_peers:
            pltpu.make_async_remote_copy(
                src_ref=src.at[p, :, rows] if along_zz else src.at[:, p, rows],
                dst_ref=dst.at[zz, :, rows] if along_zz else dst.at[:, xy, rows],
                send_sem=s_sem.at[k], recv_sem=r_sem.at[k],
                device_id={"slab": p * 8 + xy} if along_zz else {**across, "slab": zz * 8 + p}, device_id_type=MESH,
            ).start()
        if along_zz:
            pltpu.make_async_copy(src.at[zz, :, rows], dst.at[zz, :, rows], r_sem.at[k]).start()

    def arrived(dst, phase, chunk):
        ref = dst.at[:, :, pl.ds(*CHUNKS[chunk])]
        pltpu.make_async_copy(ref, ref, r_sem.at[phase * 3 + chunk]).wait()

    def sent(src, phase, chunk):
        ref = src.at[pl.ds(0, 7 if phase % 3 == 0 else 8), :, pl.ds(*CHUNKS[chunk])]
        pltpu.make_async_copy(ref, ref, s_sem.at[phase * 3 + chunk]).wait()

    low_lane = lax.broadcasted_iota(jnp.int32, (96, LN), 1) < 64

    def join(k):
        w, x = units[k]
        second[k].wait_recv()
        full[w, x, mine_rows] = part[w, x] + cross[w, x]
        third[k].start()

    def forward(k):
        w, x = units[k]
        third[k].wait_recv()
        orb[w, x, 0] = full[w, x, :NG]
        packed = full[w, x, NG:]
        turned = pltpu.roll(packed, 64, 1)
        orb[w, x, 1, :96] = jnp.where(low_lane, packed, turned)
        orb[w, x, 1, 96:] = jnp.where(low_lane, turned, packed)
        o0, o1 = orb[w, x, 0], orb[w, x, 1]
        blocks = along_z(target[x, 0] * o0, target[x, 1] * o0, target[x, 2] * o1, zmat)
        for b in range(3):
            v = left(cas, blocks[b])
            for j in range(3):
                flat1[pl.ds(row_of(w * 9 + j * 3 + b, x), SL, stride=ROWS), :] = v[j * SL : (j + 1) * SL]

    def middle(chunk):
        blocks = list(BLOCKS[chunk])
        for group in [blocks[i : i + 2] for i in range(0, len(blocks), 2)]:
            cols = [
                jnp.concatenate([in1[pl.ds(row_of(n, x), SL, stride=ROWS), :] for x in range(3)], 0) for n in group
            ]
            scale = [table[(n % 9) // 3, (n % 3) // 2] for n in group]
            v = left(xmat, jnp.concatenate(cols, 1))
            v = left(xmat_t, v * jnp.concatenate(scale, 1))
            for k, n in enumerate(group):
                for x in range(3):
                    flat2[pl.ds(row_of(n, x), SL, stride=ROWS), :] = v[x * SL : (x + 1) * SL, k * LN : (k + 1) * LN]

    def finish(w, x):
        blocks = []
        for b in range(3):
            rows = [in2[pl.ds(row_of(w * 9 + j * 3 + b, x), SL, stride=ROWS), :] for j in range(3)]
            blocks.append(left(cas, jnp.concatenate(rows, 0)))
        blocks = along_z(*blocks, zmat)
        o0, o1 = orb[w, x, 0], orb[w, x, 1]
        for b, o in enumerate((o0, o0, o1)):
            acc[x, b] = -blocks[b] * o if w == 0 else acc[x, b] - blocks[b] * o

    join(0)
    for k in range(6):
        if k < 5:
            join(k + 1)
        forward(k)
        if k == 2:
            exchange(send1, mid1, 0, 0, True)
    exchange(send1, mid1, 0, 1, True)
    exchange(send1, mid1, 0, 2, True)

    def relay1(chunk):
        arrived(mid1, 0, chunk)
        exchange(mid1, recv1, 1, chunk, False)

    def conv(chunk):
        arrived(recv1, 1, chunk)
        middle(chunk)
        exchange(send2, mid2, 2, chunk, False)

    def relay2(chunk):
        arrived(mid2, 2, chunk)
        exchange(mid2, recv2, 3, chunk, True)

    relay1(0)
    conv(0)
    relay1(1)
    conv(1)
    relay2(0)
    relay1(2)
    relay2(1)
    conv(2)
    relay2(2)
    arrived(recv2, 3, 0)
    arrived(recv2, 3, 1)
    for x in range(3):
        finish(0, x)
    arrived(recv2, 3, 2)
    for x in range(3):
        finish(1, x)
        for p in range(2):
            out[p, x] = jnp.concatenate([acc[x, p], acc[x, 2][:, p * 64 : (p + 1) * 64]], 1)

    for k in range(6):
        first[k].wait_send()
        second[k].wait_send()
        third[k].wait_send()
    for phase, src in enumerate((send1, mid1, send2, mid2)):
        for chunk in range(3):
            sent(src, phase, chunk)


def shards(bands, occupied, occ_index, band_pick):
    vmem, smem = pl.BlockSpec(memory_space=pltpu.VMEM), pl.BlockSpec(memory_space=pltpu.SMEM)
    constants = [jnp.asarray(m) for m in matrices()]
    arrays = [occupied, bands] + constants
    big = pltpu.VMEM((8, 8, ROWS, LN), F32)
    return pl.pallas_call(
        kernel,
        out_shape=jax.ShapeDtypeStruct((2, PL3, NG, NG), F32),
        in_specs=[smem, smem] + [pl.BlockSpec(memory_space=pl.ANY)] * 6,
        out_specs=vmem,
        scratch_shapes=[
            big, big, big, big, big, big,
            pltpu.VMEM((2, 3, 288, LN), F32),
            pltpu.VMEM((2, 3, 144, LN), F32),
            pltpu.VMEM((2, 3, 144, LN), F32),
            pltpu.VMEM((2, 3, 144, LN), F32),
            pltpu.VMEM((2, 3, 288, LN), F32),
            pltpu.VMEM((PL3, 3, NG, LN), F32),
            pltpu.VMEM((2, PL3, 2, NG, LN), F32),
            pltpu.VMEM((3, 2, NG, LN), F32),
            pltpu.VMEM((3, 3, NG, LN), F32),
            pltpu.VMEM(bands.shape, F32),
            pltpu.VMEM(occupied.shape, F32),
            *(pltpu.VMEM(m.shape, BF16) for m in constants),
            pltpu.SemaphoreType.DMA((6,)),
            pltpu.SemaphoreType.DMA((12,)),
            pltpu.SemaphoreType.DMA((12,)),
            pltpu.SemaphoreType.DMA((18,)),
            pltpu.SemaphoreType.DMA((18,)),
        ],
        compiler_params=pltpu.CompilerParams(
            collective_id=0, has_side_effects=True, vmem_limit_bytes=62 * 1024 * 1024
        ),
    )(occ_index, band_pick, bands, occupied, *constants)


def solution(mesh):
    placed = (P("band", "slab", None, None), P("band", "slab", None, None), P(), P("band"))
    return jax.shard_map(
        shards, mesh=mesh, in_specs=placed, out_specs=P("band", "slab", None, None), check_vma=False
    )
```

```python
import functools
import math

import jax
import jax.numpy as jnp
import numpy as np
from jax import lax
from jax.experimental import pallas as pl
from jax.experimental.pallas import tpu as pltpu
from jax.sharding import PartitionSpec as P

MESH = pl.DeviceIdType.MESH
F32, BF16 = jnp.float32, jnp.bfloat16
grid_step = 0.25
omega = 0.106
NG, SL, PL3, LN = 192, 64, 3, 128
ROWS = 56
CHUNKS = ((0, 24), (24, 16), (40, 16))
BLOCKS = (range(0, 8), range(8, 13), range(13, 18))
Z_STEPS = (1, 7, 2, 6, 3, 5, 4)
XY_STEPS = ((0, 1), (1, 3), (0, 0), (1, 0), (0, 3), (1, 1), (0, 2), (1, 2))


def row_of(n, x):
    return n * 3 + x + (1 if n >= 13 else 0)


def split_host(matrix):
    high = matrix.astype(BF16)
    low = (matrix - high.astype(np.float64)).astype(BF16)
    return np.stack([np.asarray(high), np.asarray(low)])


def matrices():
    i = np.arange(NG)
    phase = 2.0 * np.pi / NG * ((i[:, None] * i[None, :]) % NG)
    cas = np.cos(phase) + np.sin(phase)
    first, second = np.zeros((256, 256)), np.zeros((256, 256))
    a, b, c = np.arange(128), np.arange(128, 192), np.arange(192, 256)
    pos0 = np.concatenate([a, b])
    pos1 = np.concatenate([a, c])
    first[np.ix_(pos0, pos0)] = cas
    second[np.ix_(pos1, pos1)] = cas
    order = (3 * np.arange(SL)[None, :] + np.arange(PL3)[:, None]).reshape(-1)
    across = cas[:, order]
    return [split_host(m) for m in (cas, np.stack([first, second]), across, across.T)]


def halves(v):
    high = v.astype(BF16)
    return high, (v - high.astype(F32)).astype(BF16)


def dot(a, b):
    return jnp.dot(a, b, preferred_element_type=F32)


def left(m_ref, v):
    high, low = halves(v)
    return dot(m_ref[0], high) + dot(m_ref[0], low) + dot(m_ref[1], high)


def along_z(b0, b1, b2, m_ref):
    (h0, l0), (h1, l1), (h2, l2) = halves(b0), halves(b1), halves(b2)

    def one(k, h, l):
        high, low = jnp.concatenate([h, h2], 1), jnp.concatenate([l, l2], 1)
        return dot(high, m_ref[0, k]) + dot(low, m_ref[0, k]) + dot(high, m_ref[1, k])

    r0, r1 = one(0, h0, l0), one(1, h1, l1)
    return r0[:, :LN], r1[:, :LN], r0[:, LN:] + r1[:, LN:]


def signed_square(mode):
    m = jnp.where(mode <= NG // 2, mode, mode - NG).astype(F32)
    wave = 2.0 * math.pi / (NG * grid_step) * m
    return wave * wave


def screened(squares):
    nonzero = jnp.where(squares > 0, squares, jnp.ones_like(squares))
    value = 4.0 * math.pi * (1.0 - jnp.exp(-squares / (4.0 * omega * omega))) / nonzero
    return jnp.where(squares > 0, value, jnp.full_like(squares, math.pi / (omega * omega)))


def kernel(
    occ_index, band_pick, bands_in, occupied_in, cas_in, zmat_in, xmat_in, xmat_t_in, out,
    send1, mid1, recv1, send2, mid2, recv2, own, got, part, cross, full, target, orb, table, acc,
    bands, occupied, cas, zmat, xmat, xmat_t,
    load, s_sem, r_sem, xs, xr,
):
    band, slab = lax.axis_index("band"), lax.axis_index("slab")
    y_lo, core = band // 2, band % 2
    zz, xy = slab // 8, slab % 8
    pairs = (
        (occupied_in, occupied), (bands_in, bands), (cas_in, cas), (zmat_in, zmat), (xmat_in, xmat), (xmat_t_in, xmat_t)
    )
    loads = [pltpu.make_async_copy(src, dst, load.at[k]) for k, (src, dst) in enumerate(pairs)]
    for copy in loads:
        copy.start()

    z_peers = [(zz + d) % 8 for d in Z_STEPS]
    xy_peers = [((xy // 4 + dy) % 2) * 4 + (xy % 4 + dx) % 4 for dy, dx in XY_STEPS]
    partner = {"band": y_lo * 2 + (1 - core)}
    across = {"band": (1 - y_lo) * 2 + core}
    barrier = pltpu.get_barrier_semaphore()
    for where in [partner] + [{"slab": z * 8 + xy} for z in z_peers] + [{**across, "slab": zz * 8 + p} for p in xy_peers]:
        pl.semaphore_signal(barrier, inc=1, device_id=where, device_id_type=MESH)

    def pack(w):
        which = occ_index[w]
        mine = which // 4 == band
        for x in range(3):
            v = occupied[which % 4, x]
            v = jnp.where(mine, v, jnp.zeros_like(v))
            own[w, x, :NG] = v[:, :LN]
            high = v[:, LN:]
            own[w, x, NG:] = jnp.concatenate([high[:96], high[96:]], 1)

    def hop(src, dst, k, where):
        return pltpu.make_async_remote_copy(
            src_ref=src, dst_ref=dst, send_sem=xs.at[k], recv_sem=xr.at[k], device_id=where, device_id_type=MESH
        )

    half = 144
    mine_rows = pl.ds(pl.multiple_of(core * half, 8), half)
    other_rows = pl.ds(pl.multiple_of((1 - core) * half, 8), half)
    units = [(w, x) for w in range(2) for x in range(3)]
    first = [hop(own.at[w, x, other_rows], got.at[w, x], w * 3 + x, partner) for w, x in units]
    second = [hop(part.at[w, x], cross.at[w, x], 6 + w * 3 + x, across) for w, x in units]
    third = [hop(full.at[w, x, mine_rows], full.at[w, x, mine_rows], 12 + w * 3 + x, partner) for w, x in units]

    loads[0].wait()
    pack(0)
    pl.semaphore_wait(barrier, 16)
    for k in range(3):
        first[k].start()
    pack(1)
    for k in range(3, 6):
        first[k].start()
    for k, (w, x) in enumerate(units):
        first[k].wait_recv()
        part[w, x] = own[w, x, mine_rows] + got[w, x]
        second[k].start()

    loads[1].wait()
    for x in range(3):
        t0, t1 = bands[band_pick[0], x], bands[band_pick[1], x]
        target[x, 0] = t0[:, :LN]
        target[x, 1] = t1[:, :LN]
        target[x, 2] = jnp.concatenate([t0[:, LN:], t1[:, LN:]], 1)
    for copy in loads[2:]:
        copy.wait()

    for j in range(3):
        ky = signed_square(jnp.full((NG, LN), j * SL, jnp.int32) + slab)
        kx = signed_square(lax.broadcasted_iota(jnp.int32, (NG, LN), 0))
        lane = lax.broadcasted_iota(jnp.int32, (NG, LN), 1)
        for b in range(2):
            kz = signed_square(lane if b == 0 else LN + lane % 64)
            table[j, b] = screened(kx + ky + kz) * (1.0 / float(NG * NG * NG))

    flat1, in1, flat2, in2 = (r.reshape(SL * ROWS, LN) for r in (send1, recv1, send2, recv2))

    def exchange(src, dst, phase, chunk, along_zz):
        rows = pl.ds(*CHUNKS[chunk])
        k = phase * 3 + chunk
        for p in z_peers if along_zz else xy_peers:
            pltpu.make_async_remote_copy(
                src_ref=src.at[p, :, rows] if along_zz else src.at[:, p, rows],
                dst_ref=dst.at[zz, :, rows] if along_zz else dst.at[:, xy, rows],
                send_sem=s_sem.at[k], recv_sem=r_sem.at[k],
                device_id={"slab": p * 8 + xy} if along_zz else {**across, "slab": zz * 8 + p}, device_id_type=MESH,
            ).start()
        if along_zz:
            pltpu.make_async_copy(src.at[zz, :, rows], dst.at[zz, :, rows], r_sem.at[k]).start()

    def arrived(dst, phase, chunk):
        ref = dst.at[:, :, pl.ds(*CHUNKS[chunk])]
        pltpu.make_async_copy(ref, ref, r_sem.at[phase * 3 + chunk]).wait()

    def sent(src, phase, chunk):
        ref = src.at[pl.ds(0, 7 if phase % 3 == 0 else 8), :, pl.ds(*CHUNKS[chunk])]
        pltpu.make_async_copy(ref, ref, s_sem.at[phase * 3 + chunk]).wait()

    low_lane = lax.broadcasted_iota(jnp.int32, (96, LN), 1) < 64

    def join(k):
        w, x = units[k]
        second[k].wait_recv()
        full[w, x, mine_rows] = part[w, x] + cross[w, x]
        third[k].start()

    def forward(k):
        w, x = units[k]
        third[k].wait_recv()
        orb[w, x, 0] = full[w, x, :NG]
        packed = full[w, x, NG:]
        turned = pltpu.roll(packed, 64, 1)
        orb[w, x, 1, :96] = jnp.where(low_lane, packed, turned)
        orb[w, x, 1, 96:] = jnp.where(low_lane, turned, packed)
        o0, o1 = orb[w, x, 0], orb[w, x, 1]
        blocks = along_z(target[x, 0] * o0, target[x, 1] * o0, target[x, 2] * o1, zmat)
        for b in range(3):
            v = left(cas, blocks[b])
            for j in range(3):
                flat1[pl.ds(row_of(w * 9 + j * 3 + b, x), SL, stride=ROWS), :] = v[j * SL : (j + 1) * SL]

    def middle(chunk):
        blocks = list(BLOCKS[chunk])
        for group in [blocks[i : i + 2] for i in range(0, len(blocks), 2)]:
            cols = [
                jnp.concatenate([in1[pl.ds(row_of(n, x), SL, stride=ROWS), :] for x in range(3)], 0) for n in group
            ]
            scale = [table[(n % 9) // 3, (n % 3) // 2] for n in group]
            v = left(xmat, jnp.concatenate(cols, 1))
            v = left(xmat_t, v * jnp.concatenate(scale, 1))
            for k, n in enumerate(group):
                for x in range(3):
                    flat2[pl.ds(row_of(n, x), SL, stride=ROWS), :] = v[x * SL : (x + 1) * SL, k * LN : (k + 1) * LN]

    def finish(w, x):
        blocks = []
        for b in range(3):
            rows = [in2[pl.ds(row_of(w * 9 + j * 3 + b, x), SL, stride=ROWS), :] for j in range(3)]
            blocks.append(left(cas, jnp.concatenate(rows, 0)))
        blocks = along_z(*blocks, zmat)
        o0, o1 = orb[w, x, 0], orb[w, x, 1]
        for b, o in enumerate((o0, o0, o1)):
            acc[x, b] = -blocks[b] * o if w == 0 else acc[x, b] - blocks[b] * o

    join(0)
    for k in range(6):
        if k < 5:
            join(k + 1)
        forward(k)
        if k == 2:
            exchange(send1, mid1, 0, 0, True)

    def relay1(chunk):
        arrived(mid1, 0, chunk)
        exchange(mid1, recv1, 1, chunk, False)

    def conv(chunk):
        arrived(recv1, 1, chunk)
        middle(chunk)
        exchange(send2, mid2, 2, chunk, False)

    def relay2(chunk):
        arrived(mid2, 2, chunk)
        exchange(mid2, recv2, 3, chunk, True)

    sent(send1, 0, 0)
    exchange(send1, mid1, 0, 1, True)
    relay1(0)
    conv(0)
    sent(send1, 0, 1)
    exchange(send1, mid1, 0, 2, True)
    relay1(1)
    conv(1)
    sent(send1, 0, 2)
    relay2(0)
    relay1(2)
    conv(2)
    relay2(1)
    relay2(2)
    arrived(recv2, 3, 0)
    arrived(recv2, 3, 1)
    for x in range(3):
        finish(0, x)
    arrived(recv2, 3, 2)
    for x in range(3):
        finish(1, x)
        for p in range(2):
            out[p, x] = jnp.concatenate([acc[x, p], acc[x, 2][:, p * 64 : (p + 1) * 64]], 1)

    for k in range(6):
        first[k].wait_send()
        second[k].wait_send()
        third[k].wait_send()
    for phase, src in ((1, mid1), (2, send2), (3, mid2)):
        for chunk in range(3):
            sent(src, phase, chunk)


def shards(bands, occupied, occ_index, band_pick):
    vmem, smem = pl.BlockSpec(memory_space=pltpu.VMEM), pl.BlockSpec(memory_space=pltpu.SMEM)
    constants = [jnp.asarray(m) for m in matrices()]
    arrays = [occupied, bands] + constants
    big = pltpu.VMEM((8, 8, ROWS, LN), F32)
    return pl.pallas_call(
        kernel,
        out_shape=jax.ShapeDtypeStruct((2, PL3, NG, NG), F32),
        in_specs=[smem, smem] + [pl.BlockSpec(memory_space=pl.ANY)] * 6,
        out_specs=vmem,
        scratch_shapes=[
            big, big, big, big, big, big,
            pltpu.VMEM((2, 3, 288, LN), F32),
            pltpu.VMEM((2, 3, 144, LN), F32),
            pltpu.VMEM((2, 3, 144, LN), F32),
            pltpu.VMEM((2, 3, 144, LN), F32),
            pltpu.VMEM((2, 3, 288, LN), F32),
            pltpu.VMEM((PL3, 3, NG, LN), F32),
            pltpu.VMEM((2, PL3, 2, NG, LN), F32),
            pltpu.VMEM((3, 2, NG, LN), F32),
            pltpu.VMEM((3, 3, NG, LN), F32),
            pltpu.VMEM(bands.shape, F32),
            pltpu.VMEM(occupied.shape, F32),
            *(pltpu.VMEM(m.shape, BF16) for m in constants),
            pltpu.SemaphoreType.DMA((6,)),
            pltpu.SemaphoreType.DMA((12,)),
            pltpu.SemaphoreType.DMA((12,)),
            pltpu.SemaphoreType.DMA((18,)),
            pltpu.SemaphoreType.DMA((18,)),
        ],
        compiler_params=pltpu.CompilerParams(
            collective_id=0, has_side_effects=True, vmem_limit_bytes=62 * 1024 * 1024
        ),
    )(occ_index, band_pick, bands, occupied, *constants)


def solution(mesh):
    placed = (P("band", "slab", None, None), P("band", "slab", None, None), P(), P("band"))
    return jax.shard_map(
        shards, mesh=mesh, in_specs=placed, out_specs=P("band", "slab", None, None), check_vma=False
    )
```

```python
import functools
import math

import jax
import jax.numpy as jnp
import numpy as np
from jax import lax
from jax.experimental import pallas as pl
from jax.experimental.pallas import tpu as pltpu
from jax.sharding import PartitionSpec as P

MESH = pl.DeviceIdType.MESH
F32, BF16 = jnp.float32, jnp.bfloat16
grid_step = 0.25
omega = 0.106
NG, SL, PL3, LN = 192, 64, 3, 128
ROWS = 56
CHUNKS = ((0, 24), (24, 16), (40, 16))
BLOCKS = (range(0, 8), range(8, 13), range(13, 18))
WIDE = 58
Z_STEPS = (1, 7, 2, 6, 3, 5, 4)


def row_of(n, x):
    if n < 8:
        return x * 8 + n
    return 24 + x * 5 + n - 8 if n < 13 else 40 + x * 5 + n - 13


def split_host(matrix):
    high = matrix.astype(BF16)
    low = (matrix - high.astype(np.float64)).astype(BF16)
    return np.stack([np.asarray(high), np.asarray(low)])


def matrices():
    i = np.arange(NG)
    phase = 2.0 * np.pi / NG * ((i[:, None] * i[None, :]) % NG)
    cas = np.cos(phase) + np.sin(phase)
    first, second = np.zeros((256, 256)), np.zeros((256, 256))
    a, b, c = np.arange(128), np.arange(128, 192), np.arange(192, 256)
    pos0 = np.concatenate([a, b])
    pos1 = np.concatenate([a, c])
    first[np.ix_(pos0, pos0)] = cas
    second[np.ix_(pos1, pos1)] = cas
    slot = np.arange(SL)
    rows, across = [], []
    for x in range(4):
        device = slot // 4 * 4 + (x + slot % 4 - 1) % 4
        rows.append(split_host(cas[(np.arange(3)[:, None] * SL + device[None, :]).reshape(-1)]))
        across.append(split_host(cas[:, (3 * device[None, :] + np.arange(PL3)[:, None]).reshape(-1)]))
    return [np.stack(rows), split_host(np.stack([first, second])), np.stack(across)]


def halves(v):
    high = v.astype(BF16)
    return high, (v - high.astype(F32)).astype(BF16)


def dot(a, b):
    return jnp.dot(a, b, preferred_element_type=F32)


def left(m_ref, v):
    high, low = halves(v)
    return dot(m_ref[0], high) + dot(m_ref[0], low) + dot(m_ref[1], high)


def along_z(b0, b1, b2, m_ref):
    (h0, l0), (h1, l1), (h2, l2) = halves(b0), halves(b1), halves(b2)

    def one(k, h, l):
        high, low = jnp.concatenate([h, h2], 1), jnp.concatenate([l, l2], 1)
        return dot(high, m_ref[0, k]) + dot(low, m_ref[0, k]) + dot(high, m_ref[1, k])

    r0, r1 = one(0, h0, l0), one(1, h1, l1)
    return r0[:, :LN], r1[:, :LN], r0[:, LN:] + r1[:, LN:]


def signed_square(mode):
    m = jnp.where(mode <= NG // 2, mode, mode - NG).astype(F32)
    wave = 2.0 * math.pi / (NG * grid_step) * m
    return wave * wave


def screened(squares):
    nonzero = jnp.where(squares > 0, squares, jnp.ones_like(squares))
    value = 4.0 * math.pi * (1.0 - jnp.exp(-squares / (4.0 * omega * omega))) / nonzero
    return jnp.where(squares > 0, value, jnp.full_like(squares, math.pi / (omega * omega)))


def kernel(
    occ_index, band_pick, bands_in, occupied_in, rows_in, zmat_in, xmat_in, out,
    send1, mid1, recv1, send2, mid2, recv2, own, got, part, cross, full, target, orb, table, acc,
    bands, occupied, cas, zmat, xmat, cas_t, xmat_t,
    load, s_sem, r_sem, xs, xr,
):
    band, slab = lax.axis_index("band"), lax.axis_index("slab")
    y_lo, core = band // 2, band % 2
    zz, xy = slab // 8, slab % 8
    yh, xx = xy // 4, xy % 4
    pairs = (
        (occupied_in, occupied), (bands_in, bands), (rows_in.at[xx], cas), (zmat_in, zmat), (xmat_in.at[xx], xmat)
    )
    loads = [pltpu.make_async_copy(src, dst, load.at[k]) for k, (src, dst) in enumerate(pairs)]
    for copy in loads:
        copy.start()

    z_peers = [(zz + d) % 8 for d in Z_STEPS]
    up, down = (xx + 1) % 4, (xx + 3) % 4
    turn = (xx + 1 + 2 * yh) % 4
    partner = {"band": y_lo * 2 + (1 - core)}
    across = {"band": (1 - y_lo) * 2 + core}

    def at(z, y, x, **more):
        return {"slab": z * 8 + y * 4 + x, **more}

    greeted = [partner] + [at(z, yh, xx) for z in z_peers]
    greeted += [at(z, yh, x) for z in [zz] + z_peers for x in (up, down)]
    greeted += [at(zz, y, x, **across) for y in (0, 1) for x in (down, xx, up)]
    barrier = pltpu.get_barrier_semaphore()
    for where in greeted:
        pl.semaphore_signal(barrier, inc=1, device_id=where, device_id_type=MESH)

    def pack(w):
        which = occ_index[w]
        mine = which // 4 == band
        for x in range(3):
            v = occupied[which % 4, x]
            v = jnp.where(mine, v, jnp.zeros_like(v))
            own[w, x, :NG] = v[:, :LN]
            high = v[:, LN:]
            own[w, x, NG:] = jnp.concatenate([high[:96], high[96:]], 1)

    def hop(src, dst, k, where):
        return pltpu.make_async_remote_copy(
            src_ref=src, dst_ref=dst, send_sem=xs.at[k], recv_sem=xr.at[k], device_id=where, device_id_type=MESH
        )

    half = 144
    mine_rows = pl.ds(pl.multiple_of(core * half, 8), half)
    other_rows = pl.ds(pl.multiple_of((1 - core) * half, 8), half)
    units = [(w, x) for w in range(2) for x in range(3)]
    first = [hop(own.at[w, x, other_rows], got.at[w, x], w * 3 + x, partner) for w, x in units]
    second = [hop(part.at[w, x], cross.at[w, x], 6 + w * 3 + x, across) for w, x in units]
    third = [hop(full.at[w, x, mine_rows], full.at[w, x, mine_rows], 12 + w * 3 + x, partner) for w, x in units]

    loads[0].wait()
    pack(0)
    pl.semaphore_wait(barrier, len(greeted))
    for k in range(3):
        first[k].start()
    pack(1)
    for k in range(3, 6):
        first[k].start()
    for k, (w, x) in enumerate(units):
        first[k].wait_recv()
        part[w, x] = own[w, x, mine_rows] + got[w, x]
        second[k].start()

    loads[1].wait()
    for x in range(3):
        t0, t1 = bands[band_pick[0], x], bands[band_pick[1], x]
        target[x, 0] = t0[:, :LN]
        target[x, 1] = t1[:, :LN]
        target[x, 2] = jnp.concatenate([t0[:, LN:], t1[:, LN:]], 1)
    for copy in loads[2:]:
        copy.wait()
    for h in range(2):
        cas_t[h] = cas[h].astype(F32).T.astype(BF16)
        xmat_t[h] = xmat[h].astype(F32).T.astype(BF16)

    for j in range(3):
        ky = signed_square(jnp.full((NG, LN), j * SL, jnp.int32) + slab)
        kx = signed_square(lax.broadcasted_iota(jnp.int32, (NG, LN), 0))
        lane = lax.broadcasted_iota(jnp.int32, (NG, LN), 1)
        for b in range(2):
            kz = signed_square(lane if b == 0 else LN + lane % 64)
            table[j, b] = screened(kx + ky + kz) * (1.0 / float(NG * NG * NG))

    flat1, in1, flat2, in2 = (r.reshape(SL * ROWS, LN) for r in (send1, recv1, send2, recv2))

    def push(src, dst, k, where):
        pltpu.make_async_remote_copy(
            src_ref=src, dst_ref=dst, send_sem=s_sem.at[k], recv_sem=r_sem.at[k], device_id=where, device_id_type=MESH
        ).start()

    near = pl.ds(0, 3)

    def forth_z(chunk, rows):
        for z in z_peers:
            push(send1.at[z, :, near, rows], mid1.at[zz, :, near, rows], chunk, at(z, yh, xx))
            push(send1.at[z, 0, 3, rows], mid1.at[zz, 0, 3, rows], chunk, at(z, yh, up))
            push(send1.at[z, 1, 3, rows], mid1.at[zz, 1, 3, rows], chunk, at(z, yh, down))
        push(send1.at[zz, 0, 3, rows], mid1.at[zz, 0, 3, rows], chunk, at(zz, yh, up))
        push(send1.at[zz, 1, 3, rows], mid1.at[zz, 1, 3, rows], chunk, at(zz, yh, down))
        pltpu.make_async_copy(
            send1.at[zz, :, near, rows], mid1.at[zz, :, near, rows], r_sem.at[chunk]
        ).start()

    def forth_xy(chunk):
        rows, k = pl.ds(*CHUNKS[chunk]), 3 + chunk
        for r, x in ((0, down), (2, up), (1, xx)):
            for y in range(2):
                push(mid1.at[:, y, r, rows], recv1.at[:, yh, 2 - r, rows], k, at(zz, y, x, **across))
        push(mid1.at[:, 0, 3, rows], recv1.at[:, yh, 3, rows], k, at(zz, 0, up, **across))
        push(mid1.at[:, 1, 3, rows], recv1.at[:, yh, 3, rows], k, at(zz, 1, down, **across))

    def back_xy(chunk):
        rows, k = pl.ds(*CHUNKS[chunk]), 6 + chunk
        for r, x in ((0, down), (2, up), (1, xx)):
            for y in range(2):
                push(send2.at[:, y, r, rows], mid2.at[:, yh, 2 - r, rows], k, at(zz, y, x, **across))
        push(send2.at[:, 0, 3, rows], mid2.at[:, yh, 3, rows], k, at(zz, 0, up, **across))
        push(send2.at[:, 1, 3, rows], mid2.at[:, yh, 3, rows], k, at(zz, 1, down, **across))

    def back_z(chunk):
        rows, k = pl.ds(*CHUNKS[chunk]), 9 + chunk
        for z in z_peers:
            push(mid2.at[z, :, near, rows], recv2.at[zz, :, near, rows], k, at(z, yh, xx))
            push(mid2.at[z, :, 3, rows], recv2.at[zz, :, 3, rows], k, at(z, yh, turn))
        push(mid2.at[zz, :, 3, rows], recv2.at[zz, :, 3, rows], k, at(zz, yh, turn))
        pltpu.make_async_copy(mid2.at[zz, :, near, rows], recv2.at[zz, :, near, rows], r_sem.at[k]).start()

    def arrived(phase, chunk):
        ref = (mid1, recv1, mid2, recv2)[phase].at[:, :, :, pl.ds(*CHUNKS[chunk])]
        pltpu.make_async_copy(ref, ref, r_sem.at[phase * 3 + chunk]).wait()

    def sent(phase, chunk):
        ref = (send1, mid1, send2, mid2)[phase].reshape(SL, ROWS, LN)
        ref = ref.at[pl.ds(0, WIDE if phase % 3 == 0 else SL), pl.ds(*CHUNKS[chunk])]
        pltpu.make_async_copy(ref, ref, s_sem.at[phase * 3 + chunk]).wait()

    low_lane = lax.broadcasted_iota(jnp.int32, (96, LN), 1) < 64

    def join(k):
        w, x = units[k]
        second[k].wait_recv()
        full[w, x, mine_rows] = part[w, x] + cross[w, x]
        third[k].start()

    def forward(k):
        w, x = units[k]
        third[k].wait_recv()
        orb[w, x, 0] = full[w, x, :NG]
        packed = full[w, x, NG:]
        turned = pltpu.roll(packed, 64, 1)
        orb[w, x, 1, :96] = jnp.where(low_lane, packed, turned)
        orb[w, x, 1, 96:] = jnp.where(low_lane, turned, packed)
        o0, o1 = orb[w, x, 0], orb[w, x, 1]
        blocks = along_z(target[x, 0] * o0, target[x, 1] * o0, target[x, 2] * o1, zmat)
        for b in range(3):
            v = left(cas, blocks[b])
            for j in range(3):
                flat1[pl.ds(row_of(w * 9 + j * 3 + b, x), SL, stride=ROWS), :] = v[j * SL : (j + 1) * SL]

    def middle(chunk):
        blocks = list(BLOCKS[chunk])
        for group in [blocks[i : i + 2] for i in range(0, len(blocks), 2)]:
            cols = [
                jnp.concatenate([in1[pl.ds(row_of(n, x), SL, stride=ROWS), :] for x in range(3)], 0) for n in group
            ]
            scale = [table[(n % 9) // 3, (n % 3) // 2] for n in group]
            v = left(xmat, jnp.concatenate(cols, 1))
            v = left(xmat_t, v * jnp.concatenate(scale, 1))
            for k, n in enumerate(group):
                for x in range(3):
                    flat2[pl.ds(row_of(n, x), SL, stride=ROWS), :] = v[x * SL : (x + 1) * SL, k * LN : (k + 1) * LN]

    def finish(w, x):
        blocks = []
        for b in range(3):
            rows = [in2[pl.ds(row_of(w * 9 + j * 3 + b, x), SL, stride=ROWS), :] for j in range(3)]
            blocks.append(left(cas_t, jnp.concatenate(rows, 0)))
        blocks = along_z(*blocks, zmat)
        o0, o1 = orb[w, x, 0], orb[w, x, 1]
        for b, o in enumerate((o0, o0, o1)):
            acc[x, b] = -blocks[b] * o if w == 0 else acc[x, b] - blocks[b] * o

    join(0)
    for k in range(6):
        if k < 5:
            join(k + 1)
        forward(k)
        if k < 3:
            forth_z(0, pl.ds(8 * k, 8))

    def conv(chunk):
        arrived(1, chunk)
        middle(chunk)
        back_xy(chunk)

    sent(0, 0)
    forth_z(1, pl.ds(*CHUNKS[1]))
    arrived(0, 0)
    forth_xy(0)
    conv(0)
    sent(0, 1)
    forth_z(2, pl.ds(*CHUNKS[2]))
    arrived(2, 0)
    back_z(0)
    arrived(0, 1)
    forth_xy(1)
    arrived(0, 2)
    forth_xy(2)
    conv(1)
    conv(2)
    arrived(2, 1)
    back_z(1)
    arrived(2, 2)
    back_z(2)
    arrived(3, 0)
    arrived(3, 1)
    for x in range(3):
        finish(0, x)
    arrived(3, 2)
    for x in range(3):
        finish(1, x)
        for p in range(2):
            out[p, x] = jnp.concatenate([acc[x, p], acc[x, 2][:, p * 64 : (p + 1) * 64]], 1)

    for k in range(6):
        first[k].wait_send()
        second[k].wait_send()
        third[k].wait_send()
    sent(0, 2)
    for phase in range(1, 4):
        for chunk in range(3):
            sent(phase, chunk)


def shards(bands, occupied, occ_index, band_pick):
    vmem, smem = pl.BlockSpec(memory_space=pltpu.VMEM), pl.BlockSpec(memory_space=pltpu.SMEM)
    constants = [jnp.asarray(m) for m in matrices()]
    arrays = [occupied, bands] + constants
    big = pltpu.VMEM((8, 2, 4, ROWS, LN), F32)
    return pl.pallas_call(
        kernel,
        out_shape=jax.ShapeDtypeStruct((2, PL3, NG, NG), F32),
        in_specs=[smem, smem] + [pl.BlockSpec(memory_space=pl.ANY)] * 5,
        out_specs=vmem,
        scratch_shapes=[
            big, big, big, big, big, big,
            pltpu.VMEM((2, 3, 288, LN), F32),
            pltpu.VMEM((2, 3, 144, LN), F32),
            pltpu.VMEM((2, 3, 144, LN), F32),
            pltpu.VMEM((2, 3, 144, LN), F32),
            pltpu.VMEM((2, 3, 288, LN), F32),
            pltpu.VMEM((PL3, 3, NG, LN), F32),
            pltpu.VMEM((2, PL3, 2, NG, LN), F32),
            pltpu.VMEM((3, 2, NG, LN), F32),
            pltpu.VMEM((3, 3, NG, LN), F32),
            pltpu.VMEM(bands.shape, F32),
            pltpu.VMEM(occupied.shape, F32),
            pltpu.VMEM((2, NG, NG), BF16),
            pltpu.VMEM((2, 2, 256, 256), BF16),
            pltpu.VMEM((2, NG, NG), BF16),
            pltpu.VMEM((2, NG, NG), BF16),
            pltpu.VMEM((2, NG, NG), BF16),
            pltpu.SemaphoreType.DMA((5,)),
            pltpu.SemaphoreType.DMA((12,)),
            pltpu.SemaphoreType.DMA((12,)),
            pltpu.SemaphoreType.DMA((18,)),
            pltpu.SemaphoreType.DMA((18,)),
        ],
        compiler_params=pltpu.CompilerParams(
            collective_id=0, has_side_effects=True, vmem_limit_bytes=62 * 1024 * 1024
        ),
    )(occ_index, band_pick, bands, occupied, *constants)


def solution(mesh):
    placed = (P("band", "slab", None, None), P("band", "slab", None, None), P(), P("band"))
    return jax.shard_map(
        shards, mesh=mesh, in_specs=placed, out_specs=P("band", "slab", None, None), check_vma=False
    )
```

```python
import functools
import math

import jax
import jax.numpy as jnp
import numpy as np
from jax import lax
from jax.experimental import pallas as pl
from jax.experimental.pallas import tpu as pltpu
from jax.sharding import PartitionSpec as P

MESH = pl.DeviceIdType.MESH
F32, BF16 = jnp.float32, jnp.bfloat16
grid_step = 0.25
omega = 0.106
NG, SL, PL3, LN = 192, 64, 3, 128
ROWS = 56
CHUNKS = ((0, 24), (24, 16), (40, 16))
BLOCKS = (range(0, 8), range(8, 13), range(13, 18))
WIDE = 58
Z_STEPS = (1, 7, 2, 6, 3, 5, 4)


def row_of(n, x):
    if n < 8:
        return x * 8 + n
    return 24 + x * 5 + n - 8 if n < 13 else 40 + x * 5 + n - 13


def split_host(matrix):
    high = matrix.astype(BF16)
    low = (matrix - high.astype(np.float64)).astype(BF16)
    return np.stack([np.asarray(high), np.asarray(low)])


def matrices():
    i = np.arange(NG)
    phase = 2.0 * np.pi / NG * ((i[:, None] * i[None, :]) % NG)
    cas = np.cos(phase) + np.sin(phase)
    first, second = np.zeros((256, 256)), np.zeros((256, 256))
    a, b, c = np.arange(128), np.arange(128, 192), np.arange(192, 256)
    pos0 = np.concatenate([a, b])
    pos1 = np.concatenate([a, c])
    first[np.ix_(pos0, pos0)] = cas
    second[np.ix_(pos1, pos1)] = cas
    slot = np.arange(SL)
    rows, across = [], []
    for x in range(4):
        device = slot // 4 * 4 + (x + slot % 4 - 1) % 4
        rows.append(split_host(cas[(np.arange(3)[:, None] * SL + device[None, :]).reshape(-1)]))
        across.append(split_host(cas[:, (3 * device[None, :] + np.arange(PL3)[:, None]).reshape(-1)]))
    return [np.stack(rows), split_host(np.stack([first, second])), np.stack(across)]


def halves(v):
    high = v.astype(BF16)
    return high, (v - high.astype(F32)).astype(BF16)


def dot(a, b):
    return jnp.dot(a, b, preferred_element_type=F32)


def left(m_ref, v):
    high, low = halves(v)
    return dot(m_ref[0], high) + dot(m_ref[0], low) + dot(m_ref[1], high)


def along_z(b0, b1, b2, m_ref):
    (h0, l0), (h1, l1), (h2, l2) = halves(b0), halves(b1), halves(b2)

    def one(k, h, l):
        high, low = jnp.concatenate([h, h2], 1), jnp.concatenate([l, l2], 1)
        return dot(high, m_ref[0, k]) + dot(low, m_ref[0, k]) + dot(high, m_ref[1, k])

    r0, r1 = one(0, h0, l0), one(1, h1, l1)
    return r0[:, :LN], r1[:, :LN], r0[:, LN:] + r1[:, LN:]


def signed_square(mode):
    m = jnp.where(mode <= NG // 2, mode, mode - NG).astype(F32)
    wave = 2.0 * math.pi / (NG * grid_step) * m
    return wave * wave


def screened(squares):
    nonzero = jnp.where(squares > 0, squares, jnp.ones_like(squares))
    value = 4.0 * math.pi * (1.0 - jnp.exp(-squares / (4.0 * omega * omega))) / nonzero
    return jnp.where(squares > 0, value, jnp.full_like(squares, math.pi / (omega * omega)))


def kernel(
    occ_index, band_pick, bands_in, occupied_in, rows_in, zmat_in, xmat_in, out,
    send1, mid1, recv1, send2, mid2, recv2, own, got, part, cross, full, target, orb, table, acc,
    bands, occupied, cas, zmat, xmat, cas_t, xmat_t,
    load, s_sem, r_sem, xs, xr,
):
    band, slab = lax.axis_index("band"), lax.axis_index("slab")
    y_lo, core = band // 2, band % 2
    zz, xy = slab // 8, slab % 8
    yh, xx = xy // 4, xy % 4
    pairs = (
        (occupied_in, occupied), (bands_in, bands), (rows_in.at[xx], cas), (zmat_in, zmat), (xmat_in.at[xx], xmat)
    )
    loads = [pltpu.make_async_copy(src, dst, load.at[k]) for k, (src, dst) in enumerate(pairs)]
    for copy in loads:
        copy.start()

    z_peers = [(zz + d) % 8 for d in Z_STEPS]
    up, down = (xx + 1) % 4, (xx + 3) % 4
    turn = (xx + 1 + 2 * yh) % 4
    partner = {"band": y_lo * 2 + (1 - core)}
    across = {"band": (1 - y_lo) * 2 + core}

    def at(z, y, x, **more):
        return {"slab": z * 8 + y * 4 + x, **more}

    greeted = [partner] + [at(z, yh, xx) for z in z_peers]
    greeted += [at(z, yh, x) for z in [zz] + z_peers for x in (up, down)]
    greeted += [at(zz, y, x, **across) for y in (0, 1) for x in (down, xx, up)]
    barrier = pltpu.get_barrier_semaphore()
    for where in greeted:
        pl.semaphore_signal(barrier, inc=1, device_id=where, device_id_type=MESH)

    def pack(w):
        which = occ_index[w]
        mine = which // 4 == band
        for x in range(3):
            v = occupied[which % 4, x]
            v = jnp.where(mine, v, jnp.zeros_like(v))
            own[w, x, :NG] = v[:, :LN]
            high = v[:, LN:]
            own[w, x, NG:] = jnp.concatenate([high[:96], high[96:]], 1)

    def hop(src, dst, k, where):
        return pltpu.make_async_remote_copy(
            src_ref=src, dst_ref=dst, send_sem=xs.at[k], recv_sem=xr.at[k], device_id=where, device_id_type=MESH
        )

    half = 144
    mine_rows = pl.ds(pl.multiple_of(core * half, 8), half)
    other_rows = pl.ds(pl.multiple_of((1 - core) * half, 8), half)
    units = [(w, x) for w in range(2) for x in range(3)]
    first = [hop(own.at[w, x, other_rows], got.at[w, x], w * 3 + x, partner) for w, x in units]
    second = [hop(part.at[w, x], cross.at[w, x], 6 + w * 3 + x, across) for w, x in units]
    third = [hop(full.at[w, x, mine_rows], full.at[w, x, mine_rows], 12 + w * 3 + x, partner) for w, x in units]

    loads[0].wait()
    pack(0)
    pl.semaphore_wait(barrier, len(greeted))
    for k in range(3):
        first[k].start()
    pack(1)
    for k in range(3, 6):
        first[k].start()
    for k, (w, x) in enumerate(units):
        first[k].wait_recv()
        part[w, x] = own[w, x, mine_rows] + got[w, x]
        second[k].start()

    loads[1].wait()
    for x in range(3):
        t0, t1 = bands[band_pick[0], x], bands[band_pick[1], x]
        target[x, 0] = t0[:, :LN]
        target[x, 1] = t1[:, :LN]
        target[x, 2] = jnp.concatenate([t0[:, LN:], t1[:, LN:]], 1)
    for copy in loads[2:]:
        copy.wait()
    for h in range(2):
        cas_t[h] = cas[h].astype(F32).T.astype(BF16)
        xmat_t[h] = xmat[h].astype(F32).T.astype(BF16)

    for j in range(3):
        ky = signed_square(jnp.full((NG, LN), j * SL, jnp.int32) + slab)
        kx = signed_square(lax.broadcasted_iota(jnp.int32, (NG, LN), 0))
        lane = lax.broadcasted_iota(jnp.int32, (NG, LN), 1)
        for b in range(2):
            kz = signed_square(lane if b == 0 else LN + lane % 64)
            table[j, b] = screened(kx + ky + kz) * (1.0 / float(NG * NG * NG))

    flat1, in1, flat2, in2 = (r.reshape(SL * ROWS, LN) for r in (send1, recv1, send2, recv2))

    def push(src, dst, k, where):
        pltpu.make_async_remote_copy(
            src_ref=src, dst_ref=dst, send_sem=s_sem.at[k], recv_sem=r_sem.at[k], device_id=where, device_id_type=MESH
        ).start()

    near = pl.ds(0, 3)

    def z_then(src, dst, k, rows):
        for z in z_peers:
            push(src.at[z, :, near, rows], dst.at[zz, :, near, rows], k, at(z, yh, xx))
            push(src.at[z, 0, 3, rows], dst.at[zz, 0, 3, rows], k, at(z, yh, up))
            push(src.at[z, 1, 3, rows], dst.at[zz, 1, 3, rows], k, at(z, yh, down))
        push(src.at[zz, 0, 3, rows], dst.at[zz, 0, 3, rows], k, at(zz, yh, up))
        push(src.at[zz, 1, 3, rows], dst.at[zz, 1, 3, rows], k, at(zz, yh, down))
        pltpu.make_async_copy(src.at[zz, :, near, rows], dst.at[zz, :, near, rows], r_sem.at[k]).start()

    def plane(src, dst, k, rows):
        for r, x in ((0, down), (2, up), (1, xx)):
            for y in range(2):
                push(src.at[:, y, r, rows], dst.at[:, yh, 2 - r, rows], k, at(zz, y, x, **across))
        push(src.at[:, 0, 3, rows], dst.at[:, yh, 3, rows], k, at(zz, 0, up, **across))
        push(src.at[:, 1, 3, rows], dst.at[:, yh, 3, rows], k, at(zz, 1, down, **across))

    def then_z(src, dst, k, rows):
        for z in z_peers:
            push(src.at[z, :, near, rows], dst.at[zz, :, near, rows], k, at(z, yh, xx))
            push(src.at[z, :, 3, rows], dst.at[zz, :, 3, rows], k, at(z, yh, turn))
        push(src.at[zz, :, 3, rows], dst.at[zz, :, 3, rows], k, at(zz, yh, turn))
        pltpu.make_async_copy(src.at[zz, :, near, rows], dst.at[zz, :, near, rows], r_sem.at[k]).start()

    stages = ((send1, mid1), (mid1, recv1), (send2, mid2), (mid2, recv2))

    def go(chunk, stage):
        along = (z_then, plane, plane, then_z) if chunk == 0 else (plane, then_z, z_then, plane)
        along[stage](*stages[stage], stage * 3 + chunk, pl.ds(*CHUNKS[chunk]))

    def arrived(chunk, stage, k=None, rows=None):
        ref = stages[stage][1].at[:, :, :, rows or pl.ds(*CHUNKS[chunk])]
        pltpu.make_async_copy(ref, ref, r_sem.at[k or stage * 3 + chunk]).wait()

    def sent(chunk, stage, k=None, rows=None):
        ref = stages[stage][0].reshape(SL, ROWS, LN)
        wide = WIDE if (stage % 3 == 0) == (chunk == 0) else SL
        ref = ref.at[pl.ds(0, wide), rows or pl.ds(*CHUNKS[chunk])]
        pltpu.make_async_copy(ref, ref, s_sem.at[k or stage * 3 + chunk]).wait()

    low_lane = lax.broadcasted_iota(jnp.int32, (96, LN), 1) < 64

    def join(k):
        w, x = units[k]
        second[k].wait_recv()
        full[w, x, mine_rows] = part[w, x] + cross[w, x]
        third[k].start()

    def forward(k):
        w, x = units[k]
        third[k].wait_recv()
        orb[w, x, 0] = full[w, x, :NG]
        packed = full[w, x, NG:]
        turned = pltpu.roll(packed, 64, 1)
        orb[w, x, 1, :96] = jnp.where(low_lane, packed, turned)
        orb[w, x, 1, 96:] = jnp.where(low_lane, turned, packed)
        o0, o1 = orb[w, x, 0], orb[w, x, 1]
        blocks = along_z(target[x, 0] * o0, target[x, 1] * o0, target[x, 2] * o1, zmat)
        for b in range(3):
            v = left(cas, blocks[b])
            for j in range(3):
                flat1[pl.ds(row_of(w * 9 + j * 3 + b, x), SL, stride=ROWS), :] = v[j * SL : (j + 1) * SL]

    def middle(chunk):
        blocks = list(BLOCKS[chunk])
        for group in [blocks[i : i + 2] for i in range(0, len(blocks), 2)]:
            cols = [
                jnp.concatenate([in1[pl.ds(row_of(n, x), SL, stride=ROWS), :] for x in range(3)], 0) for n in group
            ]
            scale = [table[(n % 9) // 3, (n % 3) // 2] for n in group]
            v = left(xmat, jnp.concatenate(cols, 1))
            v = left(xmat_t, v * jnp.concatenate(scale, 1))
            for k, n in enumerate(group):
                for x in range(3):
                    flat2[pl.ds(row_of(n, x), SL, stride=ROWS), :] = v[x * SL : (x + 1) * SL, k * LN : (k + 1) * LN]

    def finish(w, x):
        blocks = []
        for b in range(3):
            rows = [in2[pl.ds(row_of(w * 9 + j * 3 + b, x), SL, stride=ROWS), :] for j in range(3)]
            blocks.append(left(cas_t, jnp.concatenate(rows, 0)))
        blocks = along_z(*blocks, zmat)
        o0, o1 = orb[w, x, 0], orb[w, x, 1]
        for b, o in enumerate((o0, o0, o1)):
            acc[x, b] = -blocks[b] * o if w == 1 else acc[x, b] - blocks[b] * o

    join(0)
    for k in range(6):
        if k < 5:
            join(k + 1)
        forward(k)
        if k < 3:
            z_then(send1, mid1, 0, pl.ds(8 * k, 8))

    def conv(chunk):
        arrived(chunk, 1)
        middle(chunk)
        go(chunk, 2)

    go(1, 0)
    sent(1, 0)
    go(2, 0)
    arrived(1, 0)
    sent(0, 0)
    go(1, 1)
    arrived(0, 0)
    go(0, 1)
    arrived(2, 0)
    sent(1, 1)
    go(2, 1)
    conv(0)
    conv(1)
    conv(2)
    arrived(1, 2)
    go(1, 3)
    arrived(0, 2)
    for x in range(3):
        then_z(mid2, recv2, 11 + x if x else 9, pl.ds(8 * x, 8))
    arrived(2, 2)
    go(2, 3)
    arrived(1, 3)
    arrived(2, 3)
    for x in range(3):
        finish(1, x)
    for x in range(3):
        arrived(0, 3, 11 + x if x else 9, pl.ds(8 * x, 8))
        finish(0, x)
        for p in range(2):
            out[p, x] = jnp.concatenate([acc[x, p], acc[x, 2][:, p * 64 : (p + 1) * 64]], 1)

    for k in range(6):
        first[k].wait_send()
        second[k].wait_send()
        third[k].wait_send()
    for chunk, stage in ((2, 0), (0, 1), (2, 1), (0, 2), (1, 2), (2, 2), (1, 3), (2, 3)):
        sent(chunk, stage)
    for x in range(3):
        sent(0, 3, 11 + x if x else 9, pl.ds(8 * x, 8))


def shards(bands, occupied, occ_index, band_pick):
    vmem, smem = pl.BlockSpec(memory_space=pltpu.VMEM), pl.BlockSpec(memory_space=pltpu.SMEM)
    constants = [jnp.asarray(m) for m in matrices()]
    arrays = [occupied, bands] + constants
    big = pltpu.VMEM((8, 2, 4, ROWS, LN), F32)
    return pl.pallas_call(
        kernel,
        out_shape=jax.ShapeDtypeStruct((2, PL3, NG, NG), F32),
        in_specs=[smem, smem] + [pl.BlockSpec(memory_space=pl.ANY)] * 5,
        out_specs=vmem,
        scratch_shapes=[
            big, big, big, big, big, big,
            pltpu.VMEM((2, 3, 288, LN), F32),
            pltpu.VMEM((2, 3, 144, LN), F32),
            pltpu.VMEM((2, 3, 144, LN), F32),
            pltpu.VMEM((2, 3, 144, LN), F32),
            pltpu.VMEM((2, 3, 288, LN), F32),
            pltpu.VMEM((PL3, 3, NG, LN), F32),
            pltpu.VMEM((2, PL3, 2, NG, LN), F32),
            pltpu.VMEM((3, 2, NG, LN), F32),
            pltpu.VMEM((3, 3, NG, LN), F32),
            pltpu.VMEM(bands.shape, F32),
            pltpu.VMEM(occupied.shape, F32),
            pltpu.VMEM((2, NG, NG), BF16),
            pltpu.VMEM((2, 2, 256, 256), BF16),
            pltpu.VMEM((2, NG, NG), BF16),
            pltpu.VMEM((2, NG, NG), BF16),
            pltpu.VMEM((2, NG, NG), BF16),
            pltpu.SemaphoreType.DMA((5,)),
            pltpu.SemaphoreType.DMA((14,)),
            pltpu.SemaphoreType.DMA((14,)),
            pltpu.SemaphoreType.DMA((18,)),
            pltpu.SemaphoreType.DMA((18,)),
        ],
        compiler_params=pltpu.CompilerParams(
            collective_id=0, has_side_effects=True, vmem_limit_bytes=62 * 1024 * 1024
        ),
    )(occ_index, band_pick, bands, occupied, *constants)


def solution(mesh):
    placed = (P("band", "slab", None, None), P("band", "slab", None, None), P(), P("band"))
    return jax.shard_map(
        shards, mesh=mesh, in_specs=placed, out_specs=P("band", "slab", None, None), check_vma=False
    )
```

```python
import functools
import math

import jax
import jax.numpy as jnp
import numpy as np
from jax import lax
from jax.experimental import pallas as pl
from jax.experimental.pallas import tpu as pltpu
from jax.sharding import PartitionSpec as P

MESH = pl.DeviceIdType.MESH
F32, BF16 = jnp.float32, jnp.bfloat16
grid_step = 0.25
omega = 0.106
NG, SL, PL3, LN = 192, 64, 3, 128
ROWS = 56
CHUNKS = ((0, 24), (24, 15), (40, 15))
BLOCKS = (range(0, 8), range(8, 13), range(13, 18))
WIDE = 58
Z_STEPS = (1, 7, 2, 6, 3, 5, 4)


def row_of(n, x):
    if n < 8:
        return x * 8 + n
    return 24 + x * 5 + n - 8 if n < 13 else 40 + x * 5 + n - 13


def split_host(matrix):
    high = matrix.astype(BF16)
    low = (matrix - high.astype(np.float64)).astype(BF16)
    return np.stack([np.asarray(high), np.asarray(low)])


def matrices():
    i = np.arange(NG)
    phase = 2.0 * np.pi / NG * ((i[:, None] * i[None, :]) % NG)
    cas = np.cos(phase) + np.sin(phase)
    first, second = np.zeros((256, 256)), np.zeros((256, 256))
    a, b, c = np.arange(128), np.arange(128, 192), np.arange(192, 256)
    pos0 = np.concatenate([a, b])
    pos1 = np.concatenate([a, c])
    first[np.ix_(pos0, pos0)] = cas
    second[np.ix_(pos1, pos1)] = cas
    slot = np.arange(SL)
    rows, across = [], []
    for x in range(4):
        device = slot // 4 * 4 + (x + slot % 4 - 1) % 4
        rows.append(split_host(cas[(np.arange(3)[:, None] * SL + device[None, :]).reshape(-1)]))
        across.append(split_host(cas[:, (3 * device[None, :] + np.arange(PL3)[:, None]).reshape(-1)]))
    return [np.stack(rows), split_host(np.stack([first, second])), np.stack(across)]


def halves(v):
    high = v.astype(BF16)
    return high, (v - high.astype(F32)).astype(BF16)


def dot(a, b):
    return jnp.dot(a, b, preferred_element_type=F32)


def left(m_ref, v):
    high, low = halves(v)
    return dot(m_ref[0], high) + dot(m_ref[0], low) + dot(m_ref[1], high)


def along_z(b0, b1, b2, m_ref):
    (h0, l0), (h1, l1), (h2, l2) = halves(b0), halves(b1), halves(b2)

    def one(k, h, l):
        high, low = jnp.concatenate([h, h2], 1), jnp.concatenate([l, l2], 1)
        return dot(high, m_ref[0, k]) + dot(low, m_ref[0, k]) + dot(high, m_ref[1, k])

    r0, r1 = one(0, h0, l0), one(1, h1, l1)
    return r0[:, :LN], r1[:, :LN], r0[:, LN:] + r1[:, LN:]


def signed_square(mode):
    m = jnp.where(mode <= NG // 2, mode, mode - NG).astype(F32)
    wave = 2.0 * math.pi / (NG * grid_step) * m
    return wave * wave


def screened(squares):
    nonzero = jnp.where(squares > 0, squares, jnp.ones_like(squares))
    value = 4.0 * math.pi * (1.0 - jnp.exp(-squares / (4.0 * omega * omega))) / nonzero
    return jnp.where(squares > 0, value, jnp.full_like(squares, math.pi / (omega * omega)))


def kernel(
    occ_index, band_pick, bands_in, occupied_in, rows_in, zmat_in, xmat_in, out,
    send1, mid1, recv1, send2, mid2, recv2, own, got, part, cross, full, target, orb, table, acc,
    bands, occupied0, occupied1, occupied2, cas, zmat, xmat, cas_t, xmat_t,
    load, s_sem, r_sem, xs, xr,
):
    band, slab = lax.axis_index("band"), lax.axis_index("slab")
    y_lo, core = band // 2, band % 2
    zz, xy = slab // 8, slab % 8
    yh, xx = xy // 4, xy % 4
    occupied = (occupied0, occupied1, occupied2)
    pairs = (
        *((occupied_in.at[:, x], occupied[x]) for x in range(3)),
        (bands_in, bands), (rows_in.at[xx], cas), (zmat_in, zmat), (xmat_in.at[xx], xmat)
    )
    loads = [pltpu.make_async_copy(src, dst, load.at[k]) for k, (src, dst) in enumerate(pairs)]
    for copy in loads:
        copy.start()

    z_peers = [(zz + d) % 8 for d in Z_STEPS]
    up, down = (xx + 1) % 4, (xx + 3) % 4
    turn = (xx + 1 + 2 * yh) % 4
    partner = {"band": y_lo * 2 + (1 - core)}
    across = {"band": (1 - y_lo) * 2 + core}

    def at(z, y, x, **more):
        return {"slab": z * 8 + y * 4 + x, **more}

    greeted = [partner] + [at(z, yh, xx) for z in z_peers]
    greeted += [at(z, yh, x) for z in [zz] + z_peers for x in (up, down)]
    greeted += [at(zz, y, x, **across) for y in (0, 1) for x in (down, xx, up)]
    barrier = pltpu.get_barrier_semaphore()
    for where in greeted:
        pl.semaphore_signal(barrier, inc=1, device_id=where, device_id_type=MESH)

    def pack(w, x):
        which = occ_index[w]
        mine = which // 4 == band
        v = occupied[x][which % 4]
        v = jnp.where(mine, v, jnp.zeros_like(v))
        own[w, x, :NG] = v[:, :LN]
        high = v[:, LN:]
        own[w, x, NG:] = jnp.concatenate([high[:96], high[96:]], 1)

    def hop(src, dst, k, where):
        return pltpu.make_async_remote_copy(
            src_ref=src, dst_ref=dst, send_sem=xs.at[k], recv_sem=xr.at[k], device_id=where, device_id_type=MESH
        )

    half = 144
    mine_rows = pl.ds(pl.multiple_of(core * half, 8), half)
    other_rows = pl.ds(pl.multiple_of((1 - core) * half, 8), half)
    units = [(w, x) for w in range(2) for x in range(3)]
    first = [hop(own.at[w, x, other_rows], got.at[w, x], w * 3 + x, partner) for w, x in units]
    second = [hop(part.at[w, x], cross.at[w, x], 6 + w * 3 + x, across) for w, x in units]
    third = [hop(full.at[w, x, mine_rows], full.at[w, x, mine_rows], 12 + w * 3 + x, partner) for w, x in units]

    loads[0].wait()
    pack(0, 0)
    pl.semaphore_wait(barrier, len(greeted))
    first[0].start()
    for k in range(1, 6):
        w, x = units[k]
        if w == 0:
            loads[x].wait()
        pack(w, x)
        first[k].start()
    for k, (w, x) in enumerate(units):
        first[k].wait_recv()
        part[w, x] = own[w, x, mine_rows] + got[w, x]
        second[k].start()

    loads[3].wait()
    for x in range(3):
        t0, t1 = bands[band_pick[0], x], bands[band_pick[1], x]
        target[x, 0] = t0[:, :LN]
        target[x, 1] = t1[:, :LN]
        target[x, 2] = jnp.concatenate([t0[:, LN:], t1[:, LN:]], 1)
    for copy in loads[4:]:
        copy.wait()
    for h in range(2):
        cas_t[h] = cas[h].astype(F32).T.astype(BF16)
        xmat_t[h] = xmat[h].astype(F32).T.astype(BF16)

    for j in range(3):
        ky = signed_square(jnp.full((NG, LN), j * SL, jnp.int32) + slab)
        kx = signed_square(lax.broadcasted_iota(jnp.int32, (NG, LN), 0))
        lane = lax.broadcasted_iota(jnp.int32, (NG, LN), 1)
        for b in range(2):
            kz = signed_square(lane if b == 0 else LN + lane % 64)
            table[j, b] = screened(kx + ky + kz) * (1.0 / float(NG * NG * NG))

    flat1, in1, flat2, in2 = (r.reshape(SL * ROWS, LN) for r in (send1, recv1, send2, recv2))

    def push(src, dst, k, where):
        pltpu.make_async_remote_copy(
            src_ref=src, dst_ref=dst, send_sem=s_sem.at[k], recv_sem=r_sem.at[k], device_id=where, device_id_type=MESH
        ).start()

    near = pl.ds(0, 3)

    def z_then(src, dst, k, rows):
        for z in z_peers:
            push(src.at[z, :, near, rows], dst.at[zz, :, near, rows], k, at(z, yh, xx))
            push(src.at[z, 0, 3, rows], dst.at[zz, 0, 3, rows], k, at(z, yh, up))
            push(src.at[z, 1, 3, rows], dst.at[zz, 1, 3, rows], k, at(z, yh, down))
        push(src.at[zz, 0, 3, rows], dst.at[zz, 0, 3, rows], k, at(zz, yh, up))
        push(src.at[zz, 1, 3, rows], dst.at[zz, 1, 3, rows], k, at(zz, yh, down))
        pltpu.make_async_copy(src.at[zz, :, near, rows], dst.at[zz, :, near, rows], r_sem.at[k]).start()

    def plane(src, dst, k, rows):
        for r, x in ((0, down), (2, up), (1, xx)):
            for y in range(2):
                push(src.at[:, y, r, rows], dst.at[:, yh, 2 - r, rows], k, at(zz, y, x, **across))
        push(src.at[:, 0, 3, rows], dst.at[:, yh, 3, rows], k, at(zz, 0, up, **across))
        push(src.at[:, 1, 3, rows], dst.at[:, yh, 3, rows], k, at(zz, 1, down, **across))

    def then_z(src, dst, k, rows):
        for z in z_peers:
            push(src.at[z, :, near, rows], dst.at[zz, :, near, rows], k, at(z, yh, xx))
            push(src.at[z, :, 3, rows], dst.at[zz, :, 3, rows], k, at(z, yh, turn))
        push(src.at[zz, :, 3, rows], dst.at[zz, :, 3, rows], k, at(zz, yh, turn))
        pltpu.make_async_copy(src.at[zz, :, near, rows], dst.at[zz, :, near, rows], r_sem.at[k]).start()

    stages = ((send1, mid1), (mid1, recv1), (send2, mid2), (mid2, recv2))

    def go(chunk, stage):
        along = (z_then, plane, plane, then_z) if chunk == 0 else (plane, then_z, z_then, plane)
        along[stage](*stages[stage], stage * 3 + chunk, pl.ds(*CHUNKS[chunk]))

    def arrived(chunk, stage, k=None, rows=None):
        ref = stages[stage][1].at[:, :, :, rows or pl.ds(*CHUNKS[chunk])]
        pltpu.make_async_copy(ref, ref, r_sem.at[k or stage * 3 + chunk]).wait()

    def sent(chunk, stage, k=None, rows=None):
        ref = stages[stage][0].reshape(SL, ROWS, LN)
        wide = WIDE if (stage % 3 == 0) == (chunk == 0) else SL
        ref = ref.at[pl.ds(0, wide), rows or pl.ds(*CHUNKS[chunk])]
        pltpu.make_async_copy(ref, ref, s_sem.at[k or stage * 3 + chunk]).wait()

    low_lane = lax.broadcasted_iota(jnp.int32, (96, LN), 1) < 64

    def join(k):
        w, x = units[k]
        second[k].wait_recv()
        full[w, x, mine_rows] = part[w, x] + cross[w, x]
        third[k].start()

    def forward(k):
        w, x = units[k]
        third[k].wait_recv()
        orb[w, x, 0] = full[w, x, :NG]
        packed = full[w, x, NG:]
        turned = pltpu.roll(packed, 64, 1)
        orb[w, x, 1, :96] = jnp.where(low_lane, packed, turned)
        orb[w, x, 1, 96:] = jnp.where(low_lane, turned, packed)
        o0, o1 = orb[w, x, 0], orb[w, x, 1]
        blocks = along_z(target[x, 0] * o0, target[x, 1] * o0, target[x, 2] * o1, zmat)
        for b in range(3):
            v = left(cas, blocks[b])
            for j in range(3):
                flat1[pl.ds(row_of(w * 9 + j * 3 + b, x), SL, stride=ROWS), :] = v[j * SL : (j + 1) * SL]

    def middle(chunk):
        blocks = list(BLOCKS[chunk])
        for group in [blocks[i : i + 2] for i in range(0, len(blocks), 2)]:
            cols = [
                jnp.concatenate([in1[pl.ds(row_of(n, x), SL, stride=ROWS), :] for x in range(3)], 0) for n in group
            ]
            scale = [table[(n % 9) // 3, (n % 3) // 2] for n in group]
            v = left(xmat, jnp.concatenate(cols, 1))
            v = left(xmat_t, v * jnp.concatenate(scale, 1))
            for k, n in enumerate(group):
                for x in range(3):
                    flat2[pl.ds(row_of(n, x), SL, stride=ROWS), :] = v[x * SL : (x + 1) * SL, k * LN : (k + 1) * LN]

    def finish(w, x):
        blocks = []
        for b in range(3):
            rows = [in2[pl.ds(row_of(w * 9 + j * 3 + b, x), SL, stride=ROWS), :] for j in range(3)]
            blocks.append(left(cas_t, jnp.concatenate(rows, 0)))
        blocks = along_z(*blocks, zmat)
        o0, o1 = orb[w, x, 0], orb[w, x, 1]
        for b, o in enumerate((o0, o0, o1)):
            acc[x, b] = -blocks[b] * o if w == 1 else acc[x, b] - blocks[b] * o

    join(0)
    for k in range(6):
        forward(k)
        if k < 3:
            z_then(send1, mid1, 0, pl.ds(8 * k, 8))
        for j in ((1, 2), (3,), (4,), (5,), (), ())[k]:
            join(j)

    def conv(chunk):
        arrived(chunk, 1)
        middle(chunk)
        go(chunk, 2)

    go(1, 0)
    sent(1, 0)
    go(2, 0)
    arrived(1, 0)
    sent(0, 0)
    go(1, 1)
    arrived(0, 0)
    go(0, 1)
    arrived(2, 0)
    sent(1, 1)
    go(2, 1)
    conv(0)
    conv(1)
    conv(2)
    arrived(1, 2)
    go(1, 3)
    arrived(0, 2)
    for x in range(3):
        then_z(mid2, recv2, 11 + x if x else 9, pl.ds(8 * x, 8))
    arrived(2, 2)
    go(2, 3)
    arrived(1, 3)
    arrived(2, 3)
    for x in range(3):
        finish(1, x)
    for x in range(3):
        arrived(0, 3, 11 + x if x else 9, pl.ds(8 * x, 8))
        finish(0, x)
        for p in range(2):
            out[p, x] = jnp.concatenate([acc[x, p], acc[x, 2][:, p * 64 : (p + 1) * 64]], 1)

    for k in range(6):
        first[k].wait_send()
        second[k].wait_send()
        third[k].wait_send()
    for chunk, stage in ((2, 0), (0, 1), (2, 1), (0, 2), (1, 2), (2, 2), (1, 3), (2, 3)):
        sent(chunk, stage)
    for x in range(3):
        sent(0, 3, 11 + x if x else 9, pl.ds(8 * x, 8))


def shards(bands, occupied, occ_index, band_pick):
    vmem, smem = pl.BlockSpec(memory_space=pltpu.VMEM), pl.BlockSpec(memory_space=pltpu.SMEM)
    constants = [jnp.asarray(m) for m in matrices()]
    arrays = [occupied, bands] + constants
    big = pltpu.VMEM((8, 2, 4, ROWS, LN), F32)
    return pl.pallas_call(
        kernel,
        out_shape=jax.ShapeDtypeStruct((2, PL3, NG, NG), F32),
        in_specs=[smem, smem] + [pl.BlockSpec(memory_space=pl.ANY)] * 5,
        out_specs=vmem,
        scratch_shapes=[
            big, big, big, big, big, big,
            pltpu.VMEM((2, 3, 288, LN), F32),
            pltpu.VMEM((2, 3, 144, LN), F32),
            pltpu.VMEM((2, 3, 144, LN), F32),
            pltpu.VMEM((2, 3, 144, LN), F32),
            pltpu.VMEM((2, 3, 288, LN), F32),
            pltpu.VMEM((PL3, 3, NG, LN), F32),
            pltpu.VMEM((2, PL3, 2, NG, LN), F32),
            pltpu.VMEM((3, 2, NG, LN), F32),
            pltpu.VMEM((3, 3, NG, LN), F32),
            pltpu.VMEM(bands.shape, F32),
            *([pltpu.VMEM((occupied.shape[0], NG, NG), F32)] * 3),
            pltpu.VMEM((2, NG, NG), BF16),
            pltpu.VMEM((2, 2, 256, 256), BF16),
            pltpu.VMEM((2, NG, NG), BF16),
            pltpu.VMEM((2, NG, NG), BF16),
            pltpu.VMEM((2, NG, NG), BF16),
            pltpu.SemaphoreType.DMA((7,)),
            pltpu.SemaphoreType.DMA((14,)),
            pltpu.SemaphoreType.DMA((14,)),
            pltpu.SemaphoreType.DMA((18,)),
            pltpu.SemaphoreType.DMA((18,)),
        ],
        compiler_params=pltpu.CompilerParams(
            collective_id=0, has_side_effects=True, vmem_limit_bytes=40 * 1024 * 1024
        ),
    )(*(pltpu.with_memory_space_constraint(a, pltpu.HBM) for a in (occ_index, band_pick, bands, occupied, *constants)))


def solution(mesh):
    placed = (P("band", "slab", None, None), P("band", "slab", None, None), P(), P("band"))
    return jax.shard_map(
        shards, mesh=mesh, in_specs=placed, out_specs=P("band", "slab", None, None), check_vma=False
    )
```

```python
import functools
import math

import jax
import jax.numpy as jnp
import numpy as np
from jax import lax
from jax.experimental import pallas as pl
from jax.experimental.pallas import tpu as pltpu
from jax.sharding import PartitionSpec as P

MESH = pl.DeviceIdType.MESH
F32, BF16 = jnp.float32, jnp.bfloat16
grid_step = 0.25
omega = 0.106
NG, SL, PL3, LN = 192, 64, 3, 128
ROWS = 56
CHUNKS = ((0, 24), (24, 15), (40, 15))
BLOCKS = (range(0, 8), range(8, 13), range(13, 18))
WIDE = 58
Z_STEPS = (1, 7, 2, 6, 3, 5)


def row_of(n, x):
    if n < 8:
        return x * 8 + n
    return 24 + x * 5 + n - 8 if n < 13 else 40 + x * 5 + n - 13


def split_host(matrix):
    high = matrix.astype(BF16)
    low = (matrix - high.astype(np.float64)).astype(BF16)
    return np.stack([np.asarray(high), np.asarray(low)])


def matrices():
    i = np.arange(NG)
    phase = 2.0 * np.pi / NG * ((i[:, None] * i[None, :]) % NG)
    cas = np.cos(phase) + np.sin(phase)
    first, second = np.zeros((256, 256)), np.zeros((256, 256))
    a, b, c = np.arange(128), np.arange(128, 192), np.arange(192, 256)
    pos0 = np.concatenate([a, b])
    pos1 = np.concatenate([a, c])
    first[np.ix_(pos0, pos0)] = cas
    second[np.ix_(pos1, pos1)] = cas
    slot = np.arange(SL)
    rows, across = [], []
    for x in range(4):
        device = slot // 4 * 4 + (x + slot % 4 - 1) % 4
        rows.append(split_host(cas[(np.arange(3)[:, None] * SL + device[None, :]).reshape(-1)]))
        across.append(split_host(cas[(3 * device[None, :] + np.arange(PL3)[:, None]).reshape(-1)]))
    return [np.stack(rows), split_host(np.stack([first, second])), np.stack(across)]


def halves(v):
    high = v.astype(BF16)
    return high, (v - high.astype(F32)).astype(BF16)


def dot(a, b):
    return jnp.dot(a, b, preferred_element_type=F32)


def left(m_ref, v):
    high, low = halves(v)
    return dot(m_ref[0], high) + dot(m_ref[0], low) + dot(m_ref[1], high)


def along_z(b0, b1, b2, m_ref):
    (h0, l0), (h1, l1), (h2, l2) = halves(b0), halves(b1), halves(b2)

    def one(k, h, l):
        high, low = jnp.concatenate([h, h2], 1), jnp.concatenate([l, l2], 1)
        return dot(high, m_ref[0, k]) + dot(low, m_ref[0, k]) + dot(high, m_ref[1, k])

    r0, r1 = one(0, h0, l0), one(1, h1, l1)
    return r0[:, :LN], r1[:, :LN], r0[:, LN:] + r1[:, LN:]


def signed_square(mode):
    m = jnp.where(mode <= NG // 2, mode, mode - NG).astype(F32)
    wave = 2.0 * math.pi / (NG * grid_step) * m
    return wave * wave


def screened(squares):
    nonzero = jnp.where(squares > 0, squares, jnp.ones_like(squares))
    value = 4.0 * math.pi * (1.0 - jnp.exp(-squares / (4.0 * omega * omega))) / nonzero
    return jnp.where(squares > 0, value, jnp.full_like(squares, math.pi / (omega * omega)))


def kernel(
    occ_index, band_pick, bands_in, occupied_in, rows_in, zmat_in, xmat_in, out,
    send1, mid1, recv1, send2, mid2, recv2, own, got, part, cross, full, target, orb, table, acc,
    bands, occupied0, occupied1, occupied2, raw, zmat, raw_x, cas, xmat, cas_t, xmat_t, work, turned_work,
    load, s_sem, r_sem, xs, xr,
):
    band, slab = lax.axis_index("band"), lax.axis_index("slab")
    y_lo, core = band // 2, band % 2
    zz, xy = slab // 8, slab % 8
    yh, xx = xy // 4, xy % 4
    occupied = (occupied0, occupied1, occupied2)
    pairs = (
        *((occupied_in.at[:, x], occupied[x]) for x in range(3)),
        (bands_in, bands), (rows_in.at[xx], raw), (zmat_in, zmat), (xmat_in.at[xx], raw_x)
    )
    loads = [pltpu.make_async_copy(src, dst, load.at[k]) for k, (src, dst) in enumerate(pairs)]
    for copy in loads:
        copy.start()

    z_peers = [(d, (zz + d) % 8) for d in Z_STEPS]
    z_up, z_down, z_up3, z_down3 = ((zz + d) % 8 for d in (1, 7, 3, 5))
    z_turn = (zz + 1 + 6 * yh) % 8
    up, down = (xx + 1) % 4, (xx + 3) % 4
    turn = (xx + 1 + 2 * yh) % 4
    partner = {"band": y_lo * 2 + (1 - core)}
    across = {"band": (1 - y_lo) * 2 + core}

    def at(z, y, x, **more):
        return {"slab": z * 8 + y * 4 + x, **more}

    greeted = [partner] + [at(z, yh, x) for _, z in z_peers for x in (xx, up, down)]
    greeted += [at(zz, yh, x) for x in (up, down)]
    greeted += [at(z, y, x, **across) for z in (zz, z_up, z_down) for y in (0, 1) for x in (down, xx, up)]
    barrier = pltpu.get_barrier_semaphore()
    for where in greeted:
        pl.semaphore_signal(barrier, inc=1, device_id=where, device_id_type=MESH)

    def pack(w, x):
        which = occ_index[w]
        mine = which // 4 == band
        v = occupied[x][which % 4]
        v = jnp.where(mine, v, jnp.zeros_like(v))
        own[w, x, :NG] = v[:, :LN]
        high = v[:, LN:]
        own[w, x, NG:] = jnp.concatenate([high[:96], high[96:]], 1)

    def hop(src, dst, k, where):
        return pltpu.make_async_remote_copy(
            src_ref=src, dst_ref=dst, send_sem=xs.at[k], recv_sem=xr.at[k], device_id=where, device_id_type=MESH
        )

    half = 144
    mine_rows = pl.ds(pl.multiple_of(core * half, 8), half)
    other_rows = pl.ds(pl.multiple_of((1 - core) * half, 8), half)
    units = [(w, x) for w in range(2) for x in range(3)]
    first = [hop(own.at[w, x, other_rows], got.at[w, x], w * 3 + x, partner) for w, x in units]
    second = [hop(part.at[w, x], cross.at[w, x], 6 + w * 3 + x, across) for w, x in units]
    third = [hop(full.at[w, x, mine_rows], full.at[w, x, mine_rows], 12 + w * 3 + x, partner) for w, x in units]

    loads[0].wait()
    pack(0, 0)
    pl.semaphore_wait(barrier, len(greeted))
    first[0].start()
    for k in range(1, 6):
        w, x = units[k]
        if w == 0:
            loads[x].wait()
        pack(w, x)
        first[k].start()
    for k, (w, x) in enumerate(units):
        first[k].wait_recv()
        part[w, x] = own[w, x, mine_rows] + got[w, x]
        second[k].start()

    loads[3].wait()
    for x in range(3):
        t0, t1 = bands[band_pick[0], x], bands[band_pick[1], x]
        target[x, 0] = t0[:, :LN]
        target[x, 1] = t1[:, :LN]
        target[x, 2] = jnp.concatenate([t0[:, LN:], t1[:, LN:]], 1)
    for copy in loads[4:]:
        copy.wait()
    for source, rows, columns in ((raw, cas, cas_t), (raw_x, xmat_t, xmat)):
        for h in range(2):
            work[...] = source[h].astype(F32)
            for z in range(8):
                for j in range(3):
                    rolled = pl.multiple_of(j * SL + ((zz + z) % 8) * 8, 8)
                    turned_work[pl.ds(j * SL + z * 8, 8), :] = work[pl.ds(rolled, 8), :]
            rows[h] = turned_work[...].astype(BF16)
            columns[h] = turned_work[...].T.astype(BF16)

    for j in range(3):
        ky = signed_square(jnp.full((NG, LN), j * SL, jnp.int32) + slab)
        kx = signed_square(lax.broadcasted_iota(jnp.int32, (NG, LN), 0))
        lane = lax.broadcasted_iota(jnp.int32, (NG, LN), 1)
        for b in range(2):
            kz = signed_square(lane if b == 0 else LN + lane % 64)
            table[j, b] = screened(kx + ky + kz) * (1.0 / float(NG * NG * NG))

    flat1, in1, flat2, in2 = (r.reshape(SL * ROWS, LN) for r in (send1, recv1, send2, recv2))

    def push(src, dst, k, where):
        pltpu.make_async_remote_copy(
            src_ref=src, dst_ref=dst, send_sem=s_sem.at[k], recv_sem=r_sem.at[k], device_id=where, device_id_type=MESH
        ).start()

    near = pl.ds(0, 3)

    def z_then(src, dst, k, rows):
        for d, z in z_peers:
            push(src.at[d, :, near, rows], dst.at[8 - d, :, near, rows], k, at(z, yh, xx))
            push(src.at[d, 0, 3, rows], dst.at[8 - d, 0, 3, rows], k, at(z, yh, up))
            push(src.at[d, 1, 3, rows], dst.at[8 - d, 1, 3, rows], k, at(z, yh, down))
        for y, z, x in ((0, z_up3, up), (1, z_down3, down)):
            push(src.at[4, y, near, rows], dst.at[4, y, near, rows], k, at(z, yh, xx))
            push(src.at[4, y, 3, rows], dst.at[4, y, 3, rows], k, at(z, yh, x))
        push(src.at[0, 0, 3, rows], dst.at[0, 0, 3, rows], k, at(zz, yh, up))
        push(src.at[0, 1, 3, rows], dst.at[0, 1, 3, rows], k, at(zz, yh, down))
        pltpu.make_async_copy(src.at[0, :, near, rows], dst.at[0, :, near, rows], r_sem.at[k]).start()

    def plane(src, dst, k, rows, ahead):
        hops = [(y, r, 2 - r, x) for r, x in ((0, down), (2, up), (1, xx)) for y in range(2)]
        for y, r, q, x in hops + [(0, 3, 3, up), (1, 3, 3, down)]:
            z = z_turn if ahead else (z_up, z_down)[y]
            push(src.at[4, y, r, rows], dst.at[4, yh, q, rows], k, at(z, y, x, **across))
            for part in (pl.ds(0, 4), pl.ds(5, 3)):
                push(src.at[part, y, r, rows], dst.at[part, yh, q, rows], k, at(zz, y, x, **across))

    def then_z(src, dst, k, rows):
        for d, z in z_peers:
            push(src.at[d, :, near, rows], dst.at[8 - d, :, near, rows], k, at(z, yh, xx))
            push(src.at[d, :, 3, rows], dst.at[8 - d, :, 3, rows], k, at(z, yh, turn))
        for y, z in ((0, z_up3), (1, z_down3)):
            push(src.at[4, y, near, rows], dst.at[4, y, near, rows], k, at(z, yh, xx))
            push(src.at[4, y, 3, rows], dst.at[4, y, 3, rows], k, at(z, yh, turn))
        push(src.at[0, :, 3, rows], dst.at[0, :, 3, rows], k, at(zz, yh, turn))
        pltpu.make_async_copy(src.at[0, :, near, rows], dst.at[0, :, near, rows], r_sem.at[k]).start()

    plane_first, plane_last = functools.partial(plane, ahead=True), functools.partial(plane, ahead=False)
    stages = ((send1, mid1), (mid1, recv1), (send2, mid2), (mid2, recv2))

    def go(chunk, stage):
        along = (z_then, plane_last, plane_first, then_z) if chunk == 0 else (plane_first, then_z, z_then, plane_last)
        along[stage](*stages[stage], stage * 3 + chunk, pl.ds(*CHUNKS[chunk]))

    def arrived(chunk, stage, k=None, rows=None):
        ref = stages[stage][1].at[:, :, :, rows or pl.ds(*CHUNKS[chunk])]
        pltpu.make_async_copy(ref, ref, r_sem.at[k or stage * 3 + chunk]).wait()

    def sent(chunk, stage, k=None, rows=None):
        ref = stages[stage][0].reshape(SL, ROWS, LN)
        wide = WIDE if (stage % 3 == 0) == (chunk == 0) else SL
        ref = ref.at[pl.ds(0, wide), rows or pl.ds(*CHUNKS[chunk])]
        pltpu.make_async_copy(ref, ref, s_sem.at[k or stage * 3 + chunk]).wait()

    low_lane = lax.broadcasted_iota(jnp.int32, (96, LN), 1) < 64

    def join(k):
        w, x = units[k]
        second[k].wait_recv()
        full[w, x, mine_rows] = part[w, x] + cross[w, x]
        third[k].start()

    def forward(k):
        w, x = units[k]
        third[k].wait_recv()
        orb[w, x, 0] = full[w, x, :NG]
        packed = full[w, x, NG:]
        turned = pltpu.roll(packed, 64, 1)
        orb[w, x, 1, :96] = jnp.where(low_lane, packed, turned)
        orb[w, x, 1, 96:] = jnp.where(low_lane, turned, packed)
        o0, o1 = orb[w, x, 0], orb[w, x, 1]
        blocks = along_z(target[x, 0] * o0, target[x, 1] * o0, target[x, 2] * o1, zmat)
        for b in range(3):
            v = left(cas, blocks[b])
            for j in range(3):
                flat1[pl.ds(row_of(w * 9 + j * 3 + b, x), SL, stride=ROWS), :] = v[j * SL : (j + 1) * SL]

    def middle(chunk):
        blocks = list(BLOCKS[chunk])
        for group in [blocks[i : i + 2] for i in range(0, len(blocks), 2)]:
            cols = [
                jnp.concatenate([in1[pl.ds(row_of(n, x), SL, stride=ROWS), :] for x in range(3)], 0) for n in group
            ]
            scale = [table[(n % 9) // 3, (n % 3) // 2] for n in group]
            v = left(xmat, jnp.concatenate(cols, 1))
            v = left(xmat_t, v * jnp.concatenate(scale, 1))
            for k, n in enumerate(group):
                for x in range(3):
                    flat2[pl.ds(row_of(n, x), SL, stride=ROWS), :] = v[x * SL : (x + 1) * SL, k * LN : (k + 1) * LN]

    def finish(w, x):
        blocks = []
        for b in range(3):
            rows = [in2[pl.ds(row_of(w * 9 + j * 3 + b, x), SL, stride=ROWS), :] for j in range(3)]
            blocks.append(left(cas_t, jnp.concatenate(rows, 0)))
        blocks = along_z(*blocks, zmat)
        o0, o1 = orb[w, x, 0], orb[w, x, 1]
        for b, o in enumerate((o0, o0, o1)):
            acc[x, b] = -blocks[b] * o if w == 1 else acc[x, b] - blocks[b] * o

    join(0)
    for k in range(6):
        forward(k)
        if k < 3:
            z_then(send1, mid1, 0, pl.ds(8 * k, 8))
        for j in ((1, 2), (3,), (4,), (5,), (), ())[k]:
            join(j)

    def conv(chunk):
        arrived(chunk, 1)
        middle(chunk)
        go(chunk, 2)

    go(1, 0)
    sent(1, 0)
    go(2, 0)
    arrived(1, 0)
    sent(0, 0)
    go(1, 1)
    arrived(0, 0)
    go(0, 1)
    arrived(2, 0)
    sent(1, 1)
    go(2, 1)
    conv(0)
    conv(1)
    conv(2)
    arrived(1, 2)
    go(1, 3)
    arrived(0, 2)
    for x in range(3):
        then_z(mid2, recv2, 11 + x if x else 9, pl.ds(8 * x, 8))
    arrived(2, 2)
    go(2, 3)
    arrived(1, 3)
    arrived(2, 3)
    for x in range(3):
        finish(1, x)
    for x in range(3):
        arrived(0, 3, 11 + x if x else 9, pl.ds(8 * x, 8))
        finish(0, x)
        for p in range(2):
            out[p, x] = jnp.concatenate([acc[x, p], acc[x, 2][:, p * 64 : (p + 1) * 64]], 1)

    for k in range(6):
        first[k].wait_send()
        second[k].wait_send()
        third[k].wait_send()
    for chunk, stage in ((2, 0), (0, 1), (2, 1), (0, 2), (1, 2), (2, 2), (1, 3), (2, 3)):
        sent(chunk, stage)
    for x in range(3):
        sent(0, 3, 11 + x if x else 9, pl.ds(8 * x, 8))


def shards(bands, occupied, occ_index, band_pick):
    vmem, smem = pl.BlockSpec(memory_space=pltpu.VMEM), pl.BlockSpec(memory_space=pltpu.SMEM)
    constants = [jnp.asarray(m) for m in matrices()]
    arrays = [occupied, bands] + constants
    big = pltpu.VMEM((8, 2, 4, ROWS, LN), F32)
    return pl.pallas_call(
        kernel,
        out_shape=jax.ShapeDtypeStruct((2, PL3, NG, NG), F32),
        in_specs=[smem, smem] + [pl.BlockSpec(memory_space=pl.ANY)] * 5,
        out_specs=vmem,
        scratch_shapes=[
            big, big, big, big, big, big,
            pltpu.VMEM((2, 3, 288, LN), F32),
            pltpu.VMEM((2, 3, 144, LN), F32),
            pltpu.VMEM((2, 3, 144, LN), F32),
            pltpu.VMEM((2, 3, 144, LN), F32),
            pltpu.VMEM((2, 3, 288, LN), F32),
            pltpu.VMEM((PL3, 3, NG, LN), F32),
            pltpu.VMEM((2, PL3, 2, NG, LN), F32),
            pltpu.VMEM((3, 2, NG, LN), F32),
            pltpu.VMEM((3, 3, NG, LN), F32),
            pltpu.VMEM(bands.shape, F32),
            *([pltpu.VMEM((occupied.shape[0], NG, NG), F32)] * 3),
            pltpu.VMEM((2, NG, NG), BF16),
            pltpu.VMEM((2, 2, 256, 256), BF16),
            pltpu.VMEM((2, NG, NG), BF16),
            *([pltpu.VMEM((2, NG, NG), BF16)] * 4),
            *([pltpu.VMEM((NG, NG), F32)] * 2),
            pltpu.SemaphoreType.DMA((7,)),
            pltpu.SemaphoreType.DMA((14,)),
            pltpu.SemaphoreType.DMA((14,)),
            pltpu.SemaphoreType.DMA((18,)),
            pltpu.SemaphoreType.DMA((18,)),
        ],
        compiler_params=pltpu.CompilerParams(
            collective_id=0, has_side_effects=True, vmem_limit_bytes=40 * 1024 * 1024
        ),
    )(*(pltpu.with_memory_space_constraint(a, pltpu.HBM) for a in (occ_index, band_pick, bands, occupied, *constants)))


def solution(mesh):
    placed = (P("band", "slab", None, None), P("band", "slab", None, None), P(), P("band"))
    return jax.shard_map(
        shards, mesh=mesh, in_specs=placed, out_specs=P("band", "slab", None, None), check_vma=False
    )
```

```python
import functools
import math

import jax
import jax.numpy as jnp
import numpy as np
from jax import lax
from jax.experimental import pallas as pl
from jax.experimental.pallas import tpu as pltpu
from jax.sharding import PartitionSpec as P

MESH = pl.DeviceIdType.MESH
F32, BF16 = jnp.float32, jnp.bfloat16
grid_step = 0.25
omega = 0.106
NG, SL, PL3, LN = 192, 64, 3, 128
ROWS = 56
CHUNKS = ((0, 24), (24, 15), (40, 15))
BLOCKS = (range(0, 8), range(8, 13), range(13, 18))
WIDE = 56
Z_STEPS = (1, 7, 2, 6, 3, 5, 4)


def row_of(n, x):
    if n < 8:
        return x * 8 + n
    return 24 + x * 5 + n - 8 if n < 13 else 40 + x * 5 + n - 13


def split_host(matrix):
    high = matrix.astype(BF16)
    low = (matrix - high.astype(np.float64)).astype(BF16)
    return np.stack([np.asarray(high), np.asarray(low)])


def matrices():
    i = np.arange(NG)
    phase = 2.0 * np.pi / NG * ((i[:, None] * i[None, :]) % NG)
    cas = np.cos(phase) + np.sin(phase)
    first, second = np.zeros((256, 256)), np.zeros((256, 256))
    a, b, c = np.arange(128), np.arange(128, 192), np.arange(192, 256)
    pos0 = np.concatenate([a, b])
    pos1 = np.concatenate([a, c])
    first[np.ix_(pos0, pos0)] = cas
    second[np.ix_(pos1, pos1)] = cas
    slot = np.arange(SL)
    rows, across = [], []
    for x in range(4):
        device = slot // 4 * 4 + (x + slot % 4 - 1) % 4
        rows.append(split_host(cas[(np.arange(3)[:, None] * SL + device[None, :]).reshape(-1)]))
        across.append(split_host(cas[:, (3 * device[None, :] + np.arange(PL3)[:, None]).reshape(-1)]))
    return [np.stack(rows), split_host(np.stack([first, second])), np.stack(across)]


def halves(v):
    high = v.astype(BF16)
    return high, (v - high.astype(F32)).astype(BF16)


def dot(a, b):
    return jnp.dot(a, b, preferred_element_type=F32)


def left(m_ref, v):
    high, low = halves(v)
    return dot(m_ref[0], high) + dot(m_ref[0], low) + dot(m_ref[1], high)


def along_z(b0, b1, b2, m_ref):
    (h0, l0), (h1, l1), (h2, l2) = halves(b0), halves(b1), halves(b2)

    def one(k, h, l):
        high, low = jnp.concatenate([h, h2], 1), jnp.concatenate([l, l2], 1)
        return dot(high, m_ref[0, k]) + dot(low, m_ref[0, k]) + dot(high, m_ref[1, k])

    r0, r1 = one(0, h0, l0), one(1, h1, l1)
    return r0[:, :LN], r1[:, :LN], r0[:, LN:] + r1[:, LN:]


def signed_square(mode):
    m = jnp.where(mode <= NG // 2, mode, mode - NG).astype(F32)
    wave = 2.0 * math.pi / (NG * grid_step) * m
    return wave * wave


def screened(squares):
    nonzero = jnp.where(squares > 0, squares, jnp.ones_like(squares))
    value = 4.0 * math.pi * (1.0 - jnp.exp(-squares / (4.0 * omega * omega))) / nonzero
    return jnp.where(squares > 0, value, jnp.full_like(squares, math.pi / (omega * omega)))


def kernel(
    occ_index, band_pick, bands_in, occupied_in, rows_in, zmat_in, xmat_in, out,
    send1, mid1, recv1, send2, mid2, recv2, own, got, part, cross, full, target, orb, table, acc,
    bands, occupied0, occupied1, occupied2, cas, zmat, xmat, cas_t, xmat_t,
    load, s_sem, r_sem, xs, xr,
):
    band, slab = lax.axis_index("band"), lax.axis_index("slab")
    y_lo, core = band // 2, band % 2
    zz, xy = slab // 8, slab % 8
    yh, xx = xy // 4, xy % 4
    occupied = (occupied0, occupied1, occupied2)
    pairs = (
        *((occupied_in.at[:, x], occupied[x]) for x in range(3)),
        (bands_in, bands), (rows_in.at[xx], cas), (zmat_in, zmat), (xmat_in.at[xx], xmat)
    )
    loads = [pltpu.make_async_copy(src, dst, load.at[k]) for k, (src, dst) in enumerate(pairs)]
    for copy in loads:
        copy.start()

    z_peers = [(zz + d) % 8 for d in Z_STEPS]
    up, over, down = (xx + 1) % 4, (xx + 2) % 4, (xx + 3) % 4
    partner = {"band": y_lo * 2 + (1 - core)}
    across = {"band": (1 - y_lo) * 2 + core}

    def at(z, y, x, **more):
        return {"slab": z * 8 + y * 4 + x, **more}

    greeted = [partner] + [at(z, yh, xx) for z in z_peers]
    greeted += [at(zz, y, x, **across) for y in (0, 1) for x in (down, xx, up, over)]
    barrier = pltpu.get_barrier_semaphore()
    for where in greeted:
        pl.semaphore_signal(barrier, inc=1, device_id=where, device_id_type=MESH)

    def pack(w, x):
        which = occ_index[w]
        mine = which // 4 == band
        v = occupied[x][which % 4]
        v = jnp.where(mine, v, jnp.zeros_like(v))
        own[w, x, :NG] = v[:, :LN]
        high = v[:, LN:]
        own[w, x, NG:] = jnp.concatenate([high[:96], high[96:]], 1)

    def hop(src, dst, k, where):
        return pltpu.make_async_remote_copy(
            src_ref=src, dst_ref=dst, send_sem=xs.at[k], recv_sem=xr.at[k], device_id=where, device_id_type=MESH
        )

    half = 144
    mine_rows = pl.ds(pl.multiple_of(core * half, 8), half)
    other_rows = pl.ds(pl.multiple_of((1 - core) * half, 8), half)
    units = [(w, x) for w in range(2) for x in range(3)]
    first = [hop(own.at[w, x, other_rows], got.at[w, x], w * 3 + x, partner) for w, x in units]
    second = [hop(part.at[w, x], cross.at[w, x], 6 + w * 3 + x, across) for w, x in units]
    third = [hop(full.at[w, x, mine_rows], full.at[w, x, mine_rows], 12 + w * 3 + x, partner) for w, x in units]

    loads[0].wait()
    pack(0, 0)
    pl.semaphore_wait(barrier, len(greeted))
    first[0].start()
    for k in range(1, 6):
        w, x = units[k]
        if w == 0:
            loads[x].wait()
        pack(w, x)
        first[k].start()
    for k, (w, x) in enumerate(units):
        first[k].wait_recv()
        part[w, x] = own[w, x, mine_rows] + got[w, x]
        second[k].start()

    loads[3].wait()
    for x in range(3):
        t0, t1 = bands[band_pick[0], x], bands[band_pick[1], x]
        target[x, 0] = t0[:, :LN]
        target[x, 1] = t1[:, :LN]
        target[x, 2] = jnp.concatenate([t0[:, LN:], t1[:, LN:]], 1)
    for copy in loads[4:]:
        copy.wait()
    for h in range(2):
        cas_t[h] = cas[h].astype(F32).T.astype(BF16)
        xmat_t[h] = xmat[h].astype(F32).T.astype(BF16)

    for j in range(3):
        ky = signed_square(jnp.full((NG, LN), j * SL, jnp.int32) + slab)
        kx = signed_square(lax.broadcasted_iota(jnp.int32, (NG, LN), 0))
        lane = lax.broadcasted_iota(jnp.int32, (NG, LN), 1)
        for b in range(2):
            kz = signed_square(lane if b == 0 else LN + lane % 64)
            table[j, b] = screened(kx + ky + kz) * (1.0 / float(NG * NG * NG))

    flat1, in1, flat2, in2 = (r.reshape(SL * ROWS, LN) for r in (send1, recv1, send2, recv2))

    def push(src, dst, k, where):
        pltpu.make_async_remote_copy(
            src_ref=src, dst_ref=dst, send_sem=s_sem.at[k], recv_sem=r_sem.at[k], device_id=where, device_id_type=MESH
        ).start()

    def along_zz(src, dst, k, rows):
        for z in z_peers:
            push(src.at[z, :, :, rows], dst.at[zz, :, :, rows], k, at(z, yh, xx))
        pltpu.make_async_copy(src.at[zz, :, :, rows], dst.at[zz, :, :, rows], r_sem.at[k]).start()

    def plane(src, dst, k, rows):
        for r, q, x in ((0, 2, down), (2, 0, up), (3, 3, over), (1, 1, xx)):
            for y in range(2):
                push(src.at[:, y, r, rows], dst.at[:, yh, q, rows], k, at(zz, y, x, **across))

    stages = ((send1, mid1), (mid1, recv1), (send2, mid2), (mid2, recv2))

    def go(chunk, stage):
        along = (along_zz, plane, plane, along_zz) if chunk == 0 else (plane, along_zz, along_zz, plane)
        along[stage](*stages[stage], stage * 3 + chunk, pl.ds(*CHUNKS[chunk]))

    def arrived(chunk, stage, k=None, rows=None):
        ref = stages[stage][1].at[:, :, :, rows or pl.ds(*CHUNKS[chunk])]
        pltpu.make_async_copy(ref, ref, r_sem.at[k or stage * 3 + chunk]).wait()

    def sent(chunk, stage, k=None, rows=None):
        ref = stages[stage][0].reshape(SL, ROWS, LN)
        wide = WIDE if (stage % 3 == 0) == (chunk == 0) else SL
        ref = ref.at[pl.ds(0, wide), rows or pl.ds(*CHUNKS[chunk])]
        pltpu.make_async_copy(ref, ref, s_sem.at[k or stage * 3 + chunk]).wait()

    low_lane = lax.broadcasted_iota(jnp.int32, (96, LN), 1) < 64

    def join(k):
        w, x = units[k]
        second[k].wait_recv()
        full[w, x, mine_rows] = part[w, x] + cross[w, x]
        third[k].start()

    def forward(k):
        w, x = units[k]
        third[k].wait_recv()
        orb[w, x, 0] = full[w, x, :NG]
        packed = full[w, x, NG:]
        turned = pltpu.roll(packed, 64, 1)
        orb[w, x, 1, :96] = jnp.where(low_lane, packed, turned)
        orb[w, x, 1, 96:] = jnp.where(low_lane, turned, packed)
        o0, o1 = orb[w, x, 0], orb[w, x, 1]
        blocks = along_z(target[x, 0] * o0, target[x, 1] * o0, target[x, 2] * o1, zmat)
        for b in range(3):
            v = left(cas, blocks[b])
            for j in range(3):
                flat1[pl.ds(row_of(w * 9 + j * 3 + b, x), SL, stride=ROWS), :] = v[j * SL : (j + 1) * SL]

    def middle(chunk):
        blocks = list(BLOCKS[chunk])
        for group in [blocks[i : i + 2] for i in range(0, len(blocks), 2)]:
            cols = [
                jnp.concatenate([in1[pl.ds(row_of(n, x), SL, stride=ROWS), :] for x in range(3)], 0) for n in group
            ]
            scale = [table[(n % 9) // 3, (n % 3) // 2] for n in group]
            v = left(xmat, jnp.concatenate(cols, 1))
            v = left(xmat_t, v * jnp.concatenate(scale, 1))
            for k, n in enumerate(group):
                for x in range(3):
                    flat2[pl.ds(row_of(n, x), SL, stride=ROWS), :] = v[x * SL : (x + 1) * SL, k * LN : (k + 1) * LN]

    def finish(w, x):
        blocks = []
        for b in range(3):
            rows = [in2[pl.ds(row_of(w * 9 + j * 3 + b, x), SL, stride=ROWS), :] for j in range(3)]
            blocks.append(left(cas_t, jnp.concatenate(rows, 0)))
        blocks = along_z(*blocks, zmat)
        o0, o1 = orb[w, x, 0], orb[w, x, 1]
        for b, o in enumerate((o0, o0, o1)):
            acc[x, b] = -blocks[b] * o if w == 1 else acc[x, b] - blocks[b] * o

    join(0)
    for k in range(6):
        forward(k)
        if k < 3:
            along_zz(send1, mid1, 0, pl.ds(8 * k, 8))
        for j in ((1, 2), (3,), (4,), (5,), (), ())[k]:
            join(j)

    def conv(chunk):
        arrived(chunk, 1)
        middle(chunk)
        go(chunk, 2)

    go(1, 0)
    sent(1, 0)
    go(2, 0)
    arrived(1, 0)
    sent(0, 0)
    go(1, 1)
    arrived(0, 0)
    go(0, 1)
    arrived(2, 0)
    sent(1, 1)
    go(2, 1)
    conv(0)
    conv(1)
    conv(2)
    arrived(1, 2)
    go(1, 3)
    arrived(0, 2)
    for x in range(3):
        along_zz(mid2, recv2, 11 + x if x else 9, pl.ds(8 * x, 8))
    arrived(2, 2)
    go(2, 3)
    arrived(1, 3)
    arrived(2, 3)
    for x in range(3):
        finish(1, x)
    for x in range(3):
        arrived(0, 3, 11 + x if x else 9, pl.ds(8 * x, 8))
        finish(0, x)
        for p in range(2):
            out[p, x] = jnp.concatenate([acc[x, p], acc[x, 2][:, p * 64 : (p + 1) * 64]], 1)

    for k in range(6):
        first[k].wait_send()
        second[k].wait_send()
        third[k].wait_send()
    for chunk, stage in ((2, 0), (0, 1), (2, 1), (0, 2), (1, 2), (2, 2), (1, 3), (2, 3)):
        sent(chunk, stage)
    for x in range(3):
        sent(0, 3, 11 + x if x else 9, pl.ds(8 * x, 8))


def shards(bands, occupied, occ_index, band_pick):
    vmem, smem = pl.BlockSpec(memory_space=pltpu.VMEM), pl.BlockSpec(memory_space=pltpu.SMEM)
    constants = [jnp.asarray(m) for m in matrices()]
    arrays = [occupied, bands] + constants
    big = pltpu.VMEM((8, 2, 4, ROWS, LN), F32)
    return pl.pallas_call(
        kernel,
        out_shape=jax.ShapeDtypeStruct((2, PL3, NG, NG), F32),
        in_specs=[smem, smem] + [pl.BlockSpec(memory_space=pl.ANY)] * 5,
        out_specs=vmem,
        scratch_shapes=[
            big, big, big, big, big, big,
            pltpu.VMEM((2, 3, 288, LN), F32),
            pltpu.VMEM((2, 3, 144, LN), F32),
            pltpu.VMEM((2, 3, 144, LN), F32),
            pltpu.VMEM((2, 3, 144, LN), F32),
            pltpu.VMEM((2, 3, 288, LN), F32),
            pltpu.VMEM((PL3, 3, NG, LN), F32),
            pltpu.VMEM((2, PL3, 2, NG, LN), F32),
            pltpu.VMEM((3, 2, NG, LN), F32),
            pltpu.VMEM((3, 3, NG, LN), F32),
            pltpu.VMEM(bands.shape, F32),
            *([pltpu.VMEM((occupied.shape[0], NG, NG), F32)] * 3),
            pltpu.VMEM((2, NG, NG), BF16),
            pltpu.VMEM((2, 2, 256, 256), BF16),
            pltpu.VMEM((2, NG, NG), BF16),
            pltpu.VMEM((2, NG, NG), BF16),
            pltpu.VMEM((2, NG, NG), BF16),
            pltpu.SemaphoreType.DMA((7,)),
            pltpu.SemaphoreType.DMA((14,)),
            pltpu.SemaphoreType.DMA((14,)),
            pltpu.SemaphoreType.DMA((18,)),
            pltpu.SemaphoreType.DMA((18,)),
        ],
        compiler_params=pltpu.CompilerParams(
            collective_id=0, has_side_effects=True, vmem_limit_bytes=40 * 1024 * 1024
        ),
    )(*(pltpu.with_memory_space_constraint(a, pltpu.HBM) for a in (occ_index, band_pick, bands, occupied, *constants)))


def solution(mesh):
    placed = (P("band", "slab", None, None), P("band", "slab", None, None), P(), P("band"))
    return jax.shard_map(
        shards, mesh=mesh, in_specs=placed, out_specs=P("band", "slab", None, None), check_vma=False
    )
```

```python
import functools
import math

import jax
import jax.numpy as jnp
import numpy as np
from jax import lax
from jax.experimental import pallas as pl
from jax.experimental.pallas import tpu as pltpu
from jax.sharding import PartitionSpec as P

MESH = pl.DeviceIdType.MESH
F32, BF16 = jnp.float32, jnp.bfloat16
grid_step = 0.25
omega = 0.106
NG, SL, PL3, LN = 192, 64, 3, 128
ROWS = 56
CHUNKS = ((0, 24), (24, 15), (40, 15))
BLOCKS = (range(0, 8), range(8, 13), range(13, 18))
WIDE = 56
Z_STEPS = (4, 3, 5, 2, 6, 1, 7)


def row_of(n, x):
    if n < 8:
        return x * 8 + n
    return 24 + x * 5 + n - 8 if n < 13 else 40 + x * 5 + n - 13


def split_host(matrix):
    high = matrix.astype(BF16)
    low = (matrix - high.astype(np.float64)).astype(BF16)
    return np.stack([np.asarray(high), np.asarray(low)])


def matrices():
    i = np.arange(NG)
    phase = 2.0 * np.pi / NG * ((i[:, None] * i[None, :]) % NG)
    cas = np.cos(phase) + np.sin(phase)
    first, second = np.zeros((256, 256)), np.zeros((256, 256))
    a, b, c = np.arange(128), np.arange(128, 192), np.arange(192, 256)
    pos0 = np.concatenate([a, b])
    pos1 = np.concatenate([a, c])
    first[np.ix_(pos0, pos0)] = cas
    second[np.ix_(pos1, pos1)] = cas
    slot = np.arange(SL)
    rows, across = [], []
    for x in range(4):
        device = slot // 4 * 4 + (x + slot % 4 - 1) % 4
        rows.append(split_host(cas[(np.arange(3)[:, None] * SL + device[None, :]).reshape(-1)]))
        across.append(split_host(cas[:, (3 * device[None, :] + np.arange(PL3)[:, None]).reshape(-1)]))
    return [np.stack(rows), split_host(np.stack([first, second])), np.stack(across)]


def halves(v):
    high = v.astype(BF16)
    return high, (v - high.astype(F32)).astype(BF16)


def dot(a, b):
    return jnp.dot(a, b, preferred_element_type=F32)


def left(m_ref, v):
    high, low = halves(v)
    return dot(m_ref[0], high) + dot(m_ref[0], low) + dot(m_ref[1], high)


def along_z(b0, b1, b2, m_ref):
    (h0, l0), (h1, l1), (h2, l2) = halves(b0), halves(b1), halves(b2)

    def one(k, h, l):
        high, low = jnp.concatenate([h, h2], 1), jnp.concatenate([l, l2], 1)
        return dot(high, m_ref[0, k]) + dot(low, m_ref[0, k]) + dot(high, m_ref[1, k])

    r0, r1 = one(0, h0, l0), one(1, h1, l1)
    return r0[:, :LN], r1[:, :LN], r0[:, LN:] + r1[:, LN:]


def signed_square(mode):
    m = jnp.where(mode <= NG // 2, mode, mode - NG).astype(F32)
    wave = 2.0 * math.pi / (NG * grid_step) * m
    return wave * wave


def screened(squares):
    nonzero = jnp.where(squares > 0, squares, jnp.ones_like(squares))
    value = 4.0 * math.pi * (1.0 - jnp.exp(-squares / (4.0 * omega * omega))) / nonzero
    return jnp.where(squares > 0, value, jnp.full_like(squares, math.pi / (omega * omega)))


def kernel(
    occ_index, band_pick, bands_in, occupied_in, rows_in, zmat_in, xmat_in, out,
    send1, mid1, recv1, send2, mid2, recv2, own, got, part, cross, full, target, orb, table, acc,
    bands, occupied0, occupied1, occupied2, cas, zmat, xmat, cas_t, xmat_t,
    load, s_sem, r_sem, xs, xr,
):
    band, slab = lax.axis_index("band"), lax.axis_index("slab")
    y_lo, core = band // 2, band % 2
    zz, xy = slab // 8, slab % 8
    yh, xx = xy // 4, xy % 4
    occupied = (occupied0, occupied1, occupied2)
    pairs = (
        *((occupied_in.at[:, x], occupied[x]) for x in range(3)),
        (bands_in, bands), (rows_in.at[xx], cas), (zmat_in, zmat), (xmat_in.at[xx], xmat)
    )
    loads = [pltpu.make_async_copy(src, dst, load.at[k]) for k, (src, dst) in enumerate(pairs)]
    for copy in loads:
        copy.start()

    z_peers = [(zz + d) % 8 for d in Z_STEPS]
    up, over, down = (xx + 1) % 4, (xx + 2) % 4, (xx + 3) % 4
    partner = {"band": y_lo * 2 + (1 - core)}
    across = {"band": (1 - y_lo) * 2 + core}

    def at(z, y, x, **more):
        return {"slab": z * 8 + y * 4 + x, **more}

    greeted = [partner] + [at(z, yh, xx) for z in z_peers]
    greeted += [at(zz, y, x, **across) for y in (0, 1) for x in (down, xx, up, over)]
    barrier = pltpu.get_barrier_semaphore()
    for where in greeted:
        pl.semaphore_signal(barrier, inc=1, device_id=where, device_id_type=MESH)

    def pack(w, x):
        which = occ_index[w]
        mine = which // 4 == band
        v = occupied[x][which % 4]
        v = jnp.where(mine, v, jnp.zeros_like(v))
        own[w, x, :NG] = v[:, :LN]
        high = v[:, LN:]
        own[w, x, NG:] = jnp.concatenate([high[:96], high[96:]], 1)

    def hop(src, dst, k, where):
        return pltpu.make_async_remote_copy(
            src_ref=src, dst_ref=dst, send_sem=xs.at[k], recv_sem=xr.at[k], device_id=where, device_id_type=MESH
        )

    half = 144
    mine_rows = pl.ds(pl.multiple_of(core * half, 8), half)
    other_rows = pl.ds(pl.multiple_of((1 - core) * half, 8), half)
    units = [(w, x) for w in range(2) for x in range(3)]
    first = [hop(own.at[w, x, other_rows], got.at[w, x], w * 3 + x, partner) for w, x in units]
    second = [hop(part.at[w, x], cross.at[w, x], 6 + w * 3 + x, across) for w, x in units]
    third = [hop(full.at[w, x, mine_rows], full.at[w, x, mine_rows], 12 + w * 3 + x, partner) for w, x in units]

    loads[0].wait()
    pack(0, 0)
    pl.semaphore_wait(barrier, len(greeted))
    first[0].start()
    for k in range(1, 6):
        w, x = units[k]
        if w == 0:
            loads[x].wait()
        pack(w, x)
        first[k].start()
    for k, (w, x) in enumerate(units):
        first[k].wait_recv()
        part[w, x] = own[w, x, mine_rows] + got[w, x]
        second[k].start()

    loads[3].wait()
    for x in range(3):
        t0, t1 = bands[band_pick[0], x], bands[band_pick[1], x]
        target[x, 0] = t0[:, :LN]
        target[x, 1] = t1[:, :LN]
        target[x, 2] = jnp.concatenate([t0[:, LN:], t1[:, LN:]], 1)
    for copy in loads[4:]:
        copy.wait()
    for h in range(2):
        cas_t[h] = cas[h].astype(F32).T.astype(BF16)
        xmat_t[h] = xmat[h].astype(F32).T.astype(BF16)

    for j in range(3):
        ky = signed_square(jnp.full((NG, LN), j * SL, jnp.int32) + slab)
        kx = signed_square(lax.broadcasted_iota(jnp.int32, (NG, LN), 0))
        lane = lax.broadcasted_iota(jnp.int32, (NG, LN), 1)
        for b in range(2):
            kz = signed_square(lane if b == 0 else LN + lane % 64)
            table[j, b] = screened(kx + ky + kz) * (1.0 / float(NG * NG * NG))

    flat1, in1, flat2, in2 = (r.reshape(SL * ROWS, LN) for r in (send1, recv1, send2, recv2))

    def push(src, dst, k, where):
        pltpu.make_async_remote_copy(
            src_ref=src, dst_ref=dst, send_sem=s_sem.at[k], recv_sem=r_sem.at[k], device_id=where, device_id_type=MESH
        ).start()

    def along_zz(src, dst, k, rows):
        for z in z_peers:
            push(src.at[z, :, :, rows], dst.at[zz, :, :, rows], k, at(z, yh, xx))
        pltpu.make_async_copy(src.at[zz, :, :, rows], dst.at[zz, :, :, rows], r_sem.at[k]).start()

    def plane(src, dst, k, rows):
        for r, q, x in ((0, 2, down), (2, 0, up), (3, 3, over), (1, 1, xx)):
            for y in range(2):
                push(src.at[:, y, r, rows], dst.at[:, yh, q, rows], k, at(zz, y, x, **across))

    stages = ((send1, mid1), (mid1, recv1), (send2, mid2), (mid2, recv2))

    def go(chunk, stage):
        along = (along_zz, plane, plane, along_zz) if chunk == 0 else (plane, along_zz, along_zz, plane)
        along[stage](*stages[stage], stage * 3 + chunk, pl.ds(*CHUNKS[chunk]))

    def arrived(chunk, stage, k=None, rows=None):
        ref = stages[stage][1].at[:, :, :, rows or pl.ds(*CHUNKS[chunk])]
        pltpu.make_async_copy(ref, ref, r_sem.at[k or stage * 3 + chunk]).wait()

    def sent(chunk, stage, k=None, rows=None):
        ref = stages[stage][0].reshape(SL, ROWS, LN)
        wide = WIDE if (stage % 3 == 0) == (chunk == 0) else SL
        ref = ref.at[pl.ds(0, wide), rows or pl.ds(*CHUNKS[chunk])]
        pltpu.make_async_copy(ref, ref, s_sem.at[k or stage * 3 + chunk]).wait()

    low_lane = lax.broadcasted_iota(jnp.int32, (96, LN), 1) < 64

    def join(k):
        w, x = units[k]
        second[k].wait_recv()
        full[w, x, mine_rows] = part[w, x] + cross[w, x]
        third[k].start()

    def forward(k):
        w, x = units[k]
        third[k].wait_recv()
        orb[w, x, 0] = full[w, x, :NG]
        packed = full[w, x, NG:]
        turned = pltpu.roll(packed, 64, 1)
        orb[w, x, 1, :96] = jnp.where(low_lane, packed, turned)
        orb[w, x, 1, 96:] = jnp.where(low_lane, turned, packed)
        o0, o1 = orb[w, x, 0], orb[w, x, 1]
        blocks = along_z(target[x, 0] * o0, target[x, 1] * o0, target[x, 2] * o1, zmat)
        for b in range(3):
            v = left(cas, blocks[b])
            for j in range(3):
                flat1[pl.ds(row_of(w * 9 + j * 3 + b, x), SL, stride=ROWS), :] = v[j * SL : (j + 1) * SL]

    def middle(chunk):
        blocks = list(BLOCKS[chunk])
        for group in [blocks[i : i + 2] for i in range(0, len(blocks), 2)]:
            cols = [
                jnp.concatenate([in1[pl.ds(row_of(n, x), SL, stride=ROWS), :] for x in range(3)], 0) for n in group
            ]
            scale = [table[(n % 9) // 3, (n % 3) // 2] for n in group]
            v = left(xmat, jnp.concatenate(cols, 1))
            v = left(xmat_t, v * jnp.concatenate(scale, 1))
            for k, n in enumerate(group):
                for x in range(3):
                    flat2[pl.ds(row_of(n, x), SL, stride=ROWS), :] = v[x * SL : (x + 1) * SL, k * LN : (k + 1) * LN]

    def finish(w, x):
        blocks = []
        for b in range(3):
            rows = [in2[pl.ds(row_of(w * 9 + j * 3 + b, x), SL, stride=ROWS), :] for j in range(3)]
            blocks.append(left(cas_t, jnp.concatenate(rows, 0)))
        blocks = along_z(*blocks, zmat)
        o0, o1 = orb[w, x, 0], orb[w, x, 1]
        for b, o in enumerate((o0, o0, o1)):
            acc[x, b] = -blocks[b] * o if w == 1 else acc[x, b] - blocks[b] * o

    join(0)
    for k in range(6):
        forward(k)
        if k < 3:
            along_zz(send1, mid1, 0, pl.ds(8 * k, 8))
        for j in ((1, 2), (3,), (4,), (5,), (), ())[k]:
            join(j)

    def conv(chunk):
        arrived(chunk, 1)
        middle(chunk)
        go(chunk, 2)

    go(1, 0)
    sent(1, 0)
    go(2, 0)
    arrived(1, 0)
    sent(0, 0)
    go(1, 1)
    arrived(0, 0)
    go(0, 1)
    arrived(2, 0)
    sent(1, 1)
    go(2, 1)
    conv(0)
    conv(1)
    conv(2)
    arrived(1, 2)
    go(1, 3)
    arrived(0, 2)
    for x in range(3):
        along_zz(mid2, recv2, 11 + x if x else 9, pl.ds(8 * x, 8))
    arrived(2, 2)
    go(2, 3)
    arrived(1, 3)
    arrived(2, 3)
    for x in range(3):
        finish(1, x)
    for x in range(3):
        arrived(0, 3, 11 + x if x else 9, pl.ds(8 * x, 8))
        finish(0, x)
        for p in range(2):
            out[p, x] = jnp.concatenate([acc[x, p], acc[x, 2][:, p * 64 : (p + 1) * 64]], 1)

    for k in range(6):
        first[k].wait_send()
        second[k].wait_send()
        third[k].wait_send()
    for chunk, stage in ((2, 0), (0, 1), (2, 1), (0, 2), (1, 2), (2, 2), (1, 3), (2, 3)):
        sent(chunk, stage)
    for x in range(3):
        sent(0, 3, 11 + x if x else 9, pl.ds(8 * x, 8))


def shards(bands, occupied, occ_index, band_pick):
    vmem, smem = pl.BlockSpec(memory_space=pltpu.VMEM), pl.BlockSpec(memory_space=pltpu.SMEM)
    constants = [jnp.asarray(m) for m in matrices()]
    arrays = [occupied, bands] + constants
    big = pltpu.VMEM((8, 2, 4, ROWS, LN), F32)
    return pl.pallas_call(
        kernel,
        out_shape=jax.ShapeDtypeStruct((2, PL3, NG, NG), F32),
        in_specs=[smem, smem] + [pl.BlockSpec(memory_space=pl.ANY)] * 5,
        out_specs=vmem,
        scratch_shapes=[
            big, big, big, big, big, big,
            pltpu.VMEM((2, 3, 288, LN), F32),
            pltpu.VMEM((2, 3, 144, LN), F32),
            pltpu.VMEM((2, 3, 144, LN), F32),
            pltpu.VMEM((2, 3, 144, LN), F32),
            pltpu.VMEM((2, 3, 288, LN), F32),
            pltpu.VMEM((PL3, 3, NG, LN), F32),
            pltpu.VMEM((2, PL3, 2, NG, LN), F32),
            pltpu.VMEM((3, 2, NG, LN), F32),
            pltpu.VMEM((3, 3, NG, LN), F32),
            pltpu.VMEM(bands.shape, F32),
            *([pltpu.VMEM((occupied.shape[0], NG, NG), F32)] * 3),
            pltpu.VMEM((2, NG, NG), BF16),
            pltpu.VMEM((2, 2, 256, 256), BF16),
            pltpu.VMEM((2, NG, NG), BF16),
            pltpu.VMEM((2, NG, NG), BF16),
            pltpu.VMEM((2, NG, NG), BF16),
            pltpu.SemaphoreType.DMA((7,)),
            pltpu.SemaphoreType.DMA((14,)),
            pltpu.SemaphoreType.DMA((14,)),
            pltpu.SemaphoreType.DMA((18,)),
            pltpu.SemaphoreType.DMA((18,)),
        ],
        compiler_params=pltpu.CompilerParams(
            collective_id=0, has_side_effects=True, vmem_limit_bytes=40 * 1024 * 1024
        ),
    )(*(pltpu.with_memory_space_constraint(a, pltpu.HBM) for a in (occ_index, band_pick, bands, occupied, *constants)))


def solution(mesh):
    placed = (P("band", "slab", None, None), P("band", "slab", None, None), P(), P("band"))
    return jax.shard_map(
        shards, mesh=mesh, in_specs=placed, out_specs=P("band", "slab", None, None), check_vma=False
    )
```
